128 devices in a mesh: fer: 8 (over z, y_hi), bos: 16 (over y_lo, x, core).
Axes of the slice: x: 4, y: 4 (y_hi: 2, y_lo: 2; y = y_hi * 2 + y_lo), z: 4, core: 2. Of those that a mesh axis runs over, the one named last changes fastest.
Arguments:
- green: bfloat16 [4, 64, 9, 64, 128], P(None, 'fer', None, 'bos'), may hold values from -6 to 6
- bos_weight: bfloat16 [128, 9, 64, 128], P('bos'), may hold values from -12 to 12
- vertex: float32 [64, 128], P('fer', 'bos'), may hold values from 0.25 to 1.75
- block_order: int32 [16], replicated, may hold values from 0 to 15, each once
- window_start: int32 [1], replicated, may hold values from 0 to 64
Outputs:
- sigma: float32 [64, 64, 9, 128], P('bos', 'fer')
The draws below stay inside these ranges and needn't reach their ends.
Inputs may be any that keep to these rules, and one draw needn't show every extreme that they name: block_order holds every block number once.
All inputs are finite; a program needn't handle non-finite values.
Results may differ from the reference program's by a relative error of at most 0.0003.
Values may be sent and summed in bfloat16 or wider, within the bound.
A program may use at most 128 MiB of HBM per device.

```python
import jax
import jax.numpy as jnp
from jax import lax

ORBITAL_COUNT = 3
MOMENTA_FIRST = 64
MOMENTA_SECOND = 64
WB = 8
SLOT_RATIO = 4
WINDOW_FERMIONS = 64
NW = 128
NBLOCKS = 16
SPAN = 64


def block_scale(key, dims, split, least, top_value):
    loudness = 1.0
    for dim, parts in split:
        draws = jax.random.uniform(jax.random.fold_in(jax.random.fold_in(key, 6), dim), (parts,), jnp.float32, least / len(split), top_value / len(split))
        loudness = loudness * jnp.repeat(jnp.exp(draws), dims[dim] // parts).reshape((-1,) + (1,) * (len(dims) - 1 - dim))
    return loudness


def scatter_about(own_key, shape, scale, most, shards=(), held_as=jnp.bfloat16):
    drawn = scale * jax.random.normal(own_key, shape, jnp.float32)
    if shards:
        drawn = drawn * block_scale(own_key, shape, shards, -0.22, 0.18)
    return jnp.clip(drawn, -most, most).astype(held_as)


def setup_inputs(seed: int = 0) -> dict:
    key_of = jax.random.split(jax.random.key(seed), 6)
    green = scatter_about(key_of[0], (SLOT_RATIO, WINDOW_FERMIONS, ORBITAL_COUNT * ORBITAL_COUNT, MOMENTA_FIRST, 2 * MOMENTA_SECOND), 1.0, 6.0, ((1, 8), (3, 16)))
    bos_weight = scatter_about(key_of[1], (NW, ORBITAL_COUNT * ORBITAL_COUNT, MOMENTA_FIRST, 2 * MOMENTA_SECOND), 2.0, 12.0, ((0, 16),))
    vertex = jnp.clip(0.25 + 1.5 * jax.random.uniform(key_of[2], (WINDOW_FERMIONS, NW), jnp.float32) ** block_scale(key_of[2], (WINDOW_FERMIONS, NW), ((0, 8), (1, 16)), -0.2, 0.2), 0.25, 1.75)
    block_order = jax.random.permutation(key_of[3], NBLOCKS).astype(jnp.int32)
    window_start = jax.random.randint(key_of[4], (1,), 0, SPAN + 1).astype(jnp.int32)
    return {"green": green, "bos_weight": bos_weight, "vertex": vertex, "block_order": block_order, "window_start": window_start}


def complex_packed_rows(x):
    return x[..., :MOMENTA_SECOND] + 1j * x[..., MOMENTA_SECOND:]


def reference(green, bos_weight, vertex, block_order, window_start):
    green_complex = complex_packed_rows(green.astype(jnp.float32)).reshape(SLOT_RATIO * WINDOW_FERMIONS, ORBITAL_COUNT * ORBITAL_COUNT, MOMENTA_FIRST, MOMENTA_SECOND)
    start = window_start[0].astype(jnp.int32)
    window = lax.dynamic_slice_in_dim(green_complex, start, WINDOW_FERMIONS + NW, 0)
    green_r = jnp.fft.fft2(window)
    weight_r = jnp.fft.ifft2(complex_packed_rows(bos_weight.astype(jnp.float32)))
    rows = jnp.arange(NW, dtype=jnp.int32)
    omegas = (block_order[rows // WB] * WB + rows % WB).astype(jnp.int32)

    def step(total, item):
        weight_p, omega, column = item
        part = lax.dynamic_slice_in_dim(green_r, omega, WINDOW_FERMIONS, 0).reshape(WINDOW_FERMIONS, ORBITAL_COUNT, ORBITAL_COUNT, MOMENTA_FIRST, MOMENTA_SECOND)
        product = jnp.einsum('nackl,cbkl->nabkl', part, weight_p.reshape(ORBITAL_COUNT, ORBITAL_COUNT, MOMENTA_FIRST, MOMENTA_SECOND))
        return total + column[:, None, None, None, None] * product, None

    zeros = jnp.zeros((WINDOW_FERMIONS, ORBITAL_COUNT, ORBITAL_COUNT, MOMENTA_FIRST, MOMENTA_SECOND), green_r.dtype)
    total, _ = lax.scan(step, zeros, (weight_r, omegas, vertex.T))
    sigma_k = jnp.fft.ifft2(-total.reshape(WINDOW_FERMIONS, ORBITAL_COUNT * ORBITAL_COUNT, MOMENTA_FIRST, MOMENTA_SECOND))
    packed = jnp.concatenate([jnp.real(sigma_k), jnp.imag(sigma_k)], axis=-1)
    return jnp.transpose(packed, (2, 0, 1, 3))
```

```python
import functools
import math

import jax
import jax.numpy as jnp
import ml_dtypes
import numpy as np
from jax import lax
from jax.experimental import pallas as pl
from jax.experimental.pallas import tpu as pltpu
from jax.sharding import PartitionSpec as P

MESH = pl.DeviceIdType.MESH
BF16 = jnp.bfloat16
F32 = jnp.float32
L = 64
FER = 8
BOS = 16
VMEM_LIMIT = 56 * 1024 * 1024


def split_np(m):
    hi = m.astype(ml_dtypes.bfloat16)
    lo = (m - hi.astype(np.float64)).astype(ml_dtypes.bfloat16)
    return np.stack([hi, lo])


def trig(a, b):
    t = 2.0 * math.pi * ((np.asarray(a)[:, None] * np.asarray(b)[None, :]) % L) / L
    return np.cos(t), np.sin(t)


def complex_map(c, s, sign):
    m = np.zeros((2, 2) + c.shape)
    m[0, 0], m[1, 1] = c, c
    m[1, 0], m[0, 1] = -sign * s, sign * s
    return m


def first_matrix(sign, scale):
    c, s = trig(np.arange(L), np.arange(L))
    m = complex_map(c, s, sign) * scale
    return split_np(m.transpose(1, 3, 0, 2).reshape(2 * L, 2 * L))


def second_matrix(sign, scale, grouped):
    c, s = trig(np.arange(L), np.arange(L))
    m = complex_map(c, s, sign) * scale
    m = m.reshape(2, 2, L, 2, 2, 16)
    full = np.zeros((2, 2, L, 2, 2, 2, 2, 16))
    for pair in range(2):
        full[:, pair, :, :, :, pair] = m.transpose(0, 2, 3, 4, 1, 5)
    if not grouped:
        full = full.transpose(0, 1, 2, 3, 5, 6, 4, 7)
    return split_np(full.reshape(4 * L, 4 * L))


def out_x_matrix():
    c, s = trig(np.arange(L), np.arange(L))
    m = complex_map(c, s, 1.0) * (-1.0 / L)
    m = m.reshape(2, 2, 2, 2, 16, 16, 4)
    full = np.zeros((3, 16, 2, 4, 2, 2, 4, 2, 16))
    for b in range(3):
        full[b, :, :, :, :, :, b] = m.transpose(5, 1, 6, 2, 3, 0, 4)
    return split_np(full.reshape(3, 128, 512))


def out_y_matrix():
    c, s = trig(np.arange(L), np.arange(L))
    m = complex_map(c, s, 1.0) / L
    m = m.reshape(2, 2, 16, 4, L)
    full = np.zeros((4, 16, 2, 4, 4, 2, L))
    for k in range(4):
        full[:, :, :, k, k] = m.transpose(3, 2, 0, 1, 4)
    return split_np(full.reshape(512, 512))


def mm(a, b):
    return jnp.dot(a, b, preferred_element_type=F32)


def nt(a, b):
    return lax.dot_general(a, b, (((1,), (1,)), ((), ())), preferred_element_type=F32)


def halves(x):
    hi = x.astype(BF16)
    return hi, (x - hi.astype(F32)).astype(BF16)


def exchange_green(green, vertex):
    def kernel(g_ref, v_ref, x_ref, vo_ref, gs, gr, vs, vr, own):
        me = lax.axis_index("bos")
        mine = [
            pltpu.make_async_copy(g_ref.at[:, me // 8, me % 8], x_ref.at[:, :, me], own.at[0]),
            pltpu.make_async_copy(v_ref, vo_ref.at[me], own.at[1]),
        ]
        copies = []
        for i in range(1, BOS):
            to = lax.rem(me + i, BOS)
            for k, (src, dst, ss, rs) in enumerate(
                (
                    (g_ref.at[:, to // 8, lax.rem(to, 8)], x_ref.at[:, :, me], gs, gr),
                    (v_ref, vo_ref.at[me], vs, vr),
                )
            ):
                copies.append(
                    pltpu.make_async_remote_copy(
                        src_ref=src,
                        dst_ref=dst,
                        send_sem=ss.at[i],
                        recv_sem=rs.at[i],
                        device_id={"bos": to},
                        device_id_type=MESH,
                    )
                )
        for c in copies:
            c.start()
        for c in mine:
            c.start()
        for c in mine:
            c.wait()
        for c in copies:
            c.wait()

    any_ = pl.BlockSpec(memory_space=pltpu.VMEM)
    return pl.pallas_call(
        kernel,
        out_shape=(
            jax.ShapeDtypeStruct((2, 9, BOS, 4, 128), BF16),
            jax.ShapeDtypeStruct((BOS, 8, 8), F32),
        ),
        in_specs=[any_, any_],
        out_specs=(any_, any_),
        scratch_shapes=[pltpu.SemaphoreType.DMA((BOS,))] * 4 + [pltpu.SemaphoreType.DMA((2,))],
        compiler_params=pltpu.CompilerParams(has_side_effects=True),
        name="exchange_green",
    )(green, vertex)


def exchange_positions(sent):
    count = FER * BOS

    def kernel(s_ref, r_ref, ss, rs, own):
        f, j = lax.axis_index("fer"), lax.axis_index("bos")
        me = j * FER + f
        row = count - 1 - ((j // 8) * 64 + f * 8 + lax.rem(j, 8))
        mine = pltpu.make_async_copy(s_ref.at[me], r_ref.at[row], own)
        mine.start()

        def send(i, carry):
            to = lax.rem(me + i, count)
            pltpu.make_async_remote_copy(
                src_ref=s_ref.at[to],
                dst_ref=r_ref.at[row],
                send_sem=ss,
                recv_sem=rs,
                device_id={"fer": lax.rem(to, FER), "bos": to // FER},
                device_id_type=MESH,
            ).start()
            return carry

        lax.fori_loop(1, count, send, 0)
        mine.wait()
        whole = pltpu.make_async_remote_copy(
            src_ref=s_ref.at[pl.ds(0, count - 1)],
            dst_ref=r_ref.at[pl.ds(0, count - 1)],
            send_sem=ss,
            recv_sem=rs,
            device_id={"fer": f, "bos": lax.rem(j + 1, BOS)},
            device_id_type=MESH,
        )
        whole.wait()

    any_ = pl.BlockSpec(memory_space=pltpu.VMEM)
    return pl.pallas_call(
        kernel,
        out_shape=jax.ShapeDtypeStruct((count, 16, 128), F32),
        in_specs=[any_],
        out_specs=any_,
        scratch_shapes=[pltpu.SemaphoreType.DMA] * 3,
        compiler_params=pltpu.CompilerParams(has_side_effects=True, vmem_limit_bytes=VMEM_LIMIT),
        name="exchange_positions",
    )(sent)


def exchange_axis(sent, axis, size, pick, out_shape, name):
    def kernel(s_ref, r_ref, ss, rs, own):
        me = lax.axis_index(axis)
        mine = pltpu.make_async_copy(pick(s_ref, me), r_ref.at[me], own)
        copies = []
        for i in range(1, size):
            to = lax.rem(me + i, size)
            copies.append(
                pltpu.make_async_remote_copy(
                    src_ref=pick(s_ref, to),
                    dst_ref=r_ref.at[me],
                    send_sem=ss.at[i],
                    recv_sem=rs.at[i],
                    device_id={axis: to},
                    device_id_type=MESH,
                )
            )
        for c in copies:
            c.start()
        mine.start()
        mine.wait()
        for c in copies:
            c.wait()

    any_ = pl.BlockSpec(memory_space=pltpu.VMEM)
    return pl.pallas_call(
        kernel,
        out_shape=jax.ShapeDtypeStruct(out_shape, F32),
        in_specs=[any_],
        out_specs=any_,
        scratch_shapes=[pltpu.SemaphoreType.DMA((size,))] * 2 + [pltpu.SemaphoreType.DMA],
        compiler_params=pltpu.CompilerParams(has_side_effects=True),
        name=name,
    )(sent)


def to_positions(planes, weight, vertex_row, mats):
    def kernel(x_ref, w_ref, v_ref, g1, g2, w1, w2, s_ref):
        def both(x, m1, m2, row):
            z = nt(m1[0], x) + nt(m1[1], x)
            hi, lo = halves(jnp.concatenate([z[:L], z[L:]], axis=1))
            y = mm(hi, m2[0]) + mm(hi, m2[1]) + mm(lo, m2[0])
            for half in range(2):
                s_ref[:, half, row, :] = y[:, half * 128 : half * 128 + 128]

        for ac in range(9):
            both(jnp.concatenate([x_ref[0, ac], x_ref[1, ac]], axis=0), g1, g2, ac)
        for k in range(5):
            x = w_ref[0, 128 * k : 128 * k + 128] if k < 4 else w_ref[0, 512:576]
            if k == 4:
                x = jnp.concatenate([x, jnp.zeros((64, 128), BF16)], axis=0)
            both(x, w1, w2, 9 + k)
        s_ref[:, :, 14, :] = jnp.broadcast_to(v_ref[...].reshape(1, 1, 128), (L, 2, 128))
        s_ref[:, :, 15, :] = jnp.zeros((L, 2, 128), F32)

    vm = pl.BlockSpec(memory_space=pltpu.VMEM)
    return pl.pallas_call(
        kernel,
        out_shape=jax.ShapeDtypeStruct((L, 2, 16, 128), F32),
        in_specs=[vm] * 7,
        out_specs=vm,
        compiler_params=pltpu.CompilerParams(vmem_limit_bytes=VMEM_LIMIT),
        name="to_positions",
    )(planes, weight, vertex_row, *mats)


def contract(received, block_order, window_start):
    def kernel(bo, ws, r_ref, o_ref, gt, wk, wb, vert, hh, hl):
        s = ws[0]
        lane = lax.broadcasted_iota(jnp.int32, (128, 128), 1)
        for ac in range(9):
            gt[ac] = pltpu.roll(r_ref[:, ac, :].T, s, axis=1)
        for j in range(BOS):
            base = (1 - j // 8) * 64 + (7 - j % 8)
            to = pl.multiple_of(8 * (15 - bo[j]), 8)
            for k in range(5):
                wk[k, pl.ds(to, 8), :] = r_ref[pl.ds(base, 8, stride=8), 9 + k, :]
        for rg in range(2):
            for c in range(3):
                t = jnp.zeros((128, 128), F32)
                for b in range(3):
                    k, odd = divmod(3 * c + b, 2)
                    by = (32 * b - 64 * rg - 32 * odd) % 128
                    piece = wk[k]
                    if by:
                        piece = pltpu.roll(piece, by, axis=1)
                    t = jnp.where(lane // 32 == b, piece, t)
                turned = jnp.where(
                    lane % 32 < 16, -pltpu.roll(t, 112, axis=1), pltpu.roll(t, 16, axis=1)
                )
                for ri, part in enumerate((t, turned)):
                    hi, lo = halves(part)
                    rows = slice((2 * c + ri) * 128, (2 * c + ri) * 128 + 128)
                    wb[rg, rows, 0:128] = hi
                    wb[rg, rows, 128:256] = lo
        lane8 = lax.broadcasted_iota(jnp.int32, (8, 128), 1)
        raw = [r_ref[8 * (7 - o) : 8 * (7 - o) + 8, 14, :] for o in range(8)]
        turned = [jnp.zeros((8, 128), F32) for _ in range(8)]
        for j in range(BOS):
            by = lax.rem(8 * (j - bo[j]) + 128, 128)
            here = lane8 // 8 == 15 - bo[j]
            for o in range(8):
                turned[o] = jnp.where(here, pltpu.roll(raw[o], by, axis=1), turned[o])
        for o in range(8):
            vert[8 * o : 8 * o + 8, :] = turned[o]
        o_ref[...] = jnp.zeros_like(o_ref)

        row8 = lax.broadcasted_iota(jnp.int32, (8, 128), 0)
        back = s + row8
        origin = (lane8 - back + 256) % 128
        upper = [origin >= 128 - back - 8 * o for o in range(8)]

        def skewed(ac, row):
            y = jnp.broadcast_to(gt[ac, pl.ds(row, 1), :], (8, 128))
            for bit in (1, 2, 4):
                y = jnp.where(row8 & bit != 0, pltpu.roll(y, bit, axis=1), y)
            return y

        for rg in range(2):

            def step(r16, carry):
                r = rg * 16 + r16
                for a in range(3):
                    for c in range(3):
                        for ri in range(2):
                            first = skewed(3 * a + c, 64 + ri * 32 + r)
                            second = skewed(3 * a + c, ri * 32 + r)
                            octets = []
                            for o in range(8):
                                y = jnp.where(upper[o], first, second)
                                octets.append(pltpu.roll(y, 8 * o, axis=1) if o else y)
                            h = jnp.concatenate(octets, axis=0)
                            hi, lo = halves(h * vert[...])
                            at = (slice(64 * a, 64 * a + 64), slice((2 * c + ri) * 128, (2 * c + ri) * 128 + 128))
                            hh[at] = hi
                            hl[at] = lo
                acc = mm(hh[...], wb[rg]) + mm(hl[...], wb[rg])
                res = (acc[:, :128] + acc[:, 128:]).reshape(3, 64, 128)
                here = lax.broadcasted_iota(jnp.int32, (3, 64, 128), 2) % 16 == r16
                o_ref[rg] = jnp.where(here, res, o_ref[rg])
                return carry

            lax.fori_loop(0, 16, step, 0)

    vm = pl.BlockSpec(memory_space=pltpu.VMEM)
    sm = pl.BlockSpec(memory_space=pltpu.SMEM)
    return pl.pallas_call(
        kernel,
        out_shape=jax.ShapeDtypeStruct((2, 3, 64, 128), F32),
        in_specs=[sm, sm, vm],
        out_specs=vm,
        scratch_shapes=[
            pltpu.VMEM((9, 128, 128), F32),
            pltpu.VMEM((5, 128, 128), F32),
            pltpu.VMEM((2, 768, 256), BF16),
            pltpu.VMEM((64, 128), F32),
            pltpu.VMEM((192, 768), BF16),
            pltpu.VMEM((192, 768), BF16),
        ],
        compiler_params=pltpu.CompilerParams(vmem_limit_bytes=VMEM_LIMIT),
        name="contract",
    )(block_order, window_start, received)


def back_x(got, mat):
    def kernel(b_ref, m_ref, f_ref, lh, ll):
        lh[96:, :] = jnp.zeros((32, 512), BF16)
        ll[96:, :] = jnp.zeros((32, 512), BF16)
        for ryl in range(4):
            for half in range(2):
                for rg in range(2):
                    x = b_ref[2 * ryl + half, rg].reshape(24, 128)
                    hi, lo = halves(x)
                    at = (slice(24 * ryl, 24 * ryl + 24), slice((2 * half + rg) * 128, (2 * half + rg) * 128 + 128))
                    lh[at] = hi
                    ll[at] = lo
        for b in range(3):
            y = nt(m_ref[0, b], lh[...]) + nt(m_ref[0, b], ll[...]) + nt(m_ref[1, b], lh[...])
            f_ref[:, :, b * 128 : b * 128 + 128] = y.reshape(16, 8, 128)

    vm = pl.BlockSpec(memory_space=pltpu.VMEM)
    return pl.pallas_call(
        kernel,
        out_shape=jax.ShapeDtypeStruct((BOS, 8, 384), F32),
        in_specs=[vm, vm],
        out_specs=vm,
        scratch_shapes=[pltpu.VMEM((128, 512), BF16)] * 2,
        name="back_x",
    )(got, mat)


def back_y(got, mat):
    def kernel(e_ref, m_ref, o_ref, lh, ll):
        for b in range(3):
            t = e_ref[:, :, b * 128 : b * 128 + 128].reshape(128, 128).T
            hi, lo = halves(t)
            for ryl in range(4):
                at = (slice(24 * b, 24 * b + 24), slice(128 * ryl, 128 * ryl + 128))
                lh[at] = hi[24 * ryl : 24 * ryl + 24]
                ll[at] = lo[24 * ryl : 24 * ryl + 24]
        y = mm(lh[...], m_ref[0]) + mm(ll[...], m_ref[0]) + mm(lh[...], m_ref[1])
        for b in range(3):
            for a in range(3):
                for k in range(4):
                    o_ref[k, 3 * a + b] = y[24 * b + 8 * a : 24 * b + 8 * a + 8, 128 * k : 128 * k + 128]

    vm = pl.BlockSpec(memory_space=pltpu.VMEM)
    return pl.pallas_call(
        kernel,
        out_shape=jax.ShapeDtypeStruct((4, 9, 8, 128), F32),
        in_specs=[vm, vm],
        out_specs=vm,
        scratch_shapes=[pltpu.VMEM((72, 512), BF16)] * 2,
        name="back_y",
    )(got, mat)


def body(green, bos_weight, vertex, block_order, window_start):
    f, j = lax.axis_index("fer"), lax.axis_index("bos")
    planes, rows = exchange_green(green.reshape(2, 2, 8, 9, 4, 128), vertex)
    rows = rows.transpose(1, 0, 2).reshape(8, 128)[:, ::-1]
    row = lax.dynamic_slice_in_dim(rows, 7 - j % 8, 1, 0)
    weight = lax.dynamic_slice_in_dim(bos_weight, f, 1, 0).reshape(1, 576, 128)
    mats = [
        jnp.asarray(first_matrix(-1.0, 1.0)),
        jnp.asarray(second_matrix(-1.0, 1.0, False)),
        jnp.asarray(first_matrix(1.0, 1.0 / L)),
        jnp.asarray(second_matrix(1.0, 1.0 / L, True)),
    ]
    sent = to_positions(planes.reshape(2, 9, L, 128), weight, row, mats)
    got = exchange_positions(sent.reshape(128, 16, 128))
    part = contract(got, block_order, window_start)
    octets = exchange_axis(
        part, "fer", FER, lambda ref, to: ref.at[:, :, pl.ds(pl.multiple_of(8 * to, 8), 8), :], (FER, 2, 3, 8, 128), "exchange_octets"
    )
    quads = back_x(octets, jnp.asarray(out_x_matrix()))
    last = exchange_axis(quads, "bos", BOS, lambda ref, to: ref.at[to], (BOS, 8, 384), "exchange_rows")
    return back_y(last, jnp.asarray(out_y_matrix())).transpose(0, 2, 1, 3)


def solution(mesh):
    return jax.shard_map(
        body,
        mesh=mesh,
        in_specs=(
            P(None, "fer", None, "bos", None),
            P("bos", None, None, None),
            P("fer", "bos"),
            P(),
            P(),
        ),
        out_specs=P("bos", "fer", None, None),
        check_vma=False,
    )
```

```python
import functools
import math

import jax
import jax.numpy as jnp
import ml_dtypes
import numpy as np
from jax import lax
from jax.experimental import pallas as pl
from jax.experimental.pallas import tpu as pltpu
from jax.sharding import PartitionSpec as P

MESH = pl.DeviceIdType.MESH
BF16 = jnp.bfloat16
F32 = jnp.float32
L = 64
FER = 8
BOS = 16
VMEM_LIMIT = 56 * 1024 * 1024


def split_np(m):
    hi = m.astype(ml_dtypes.bfloat16)
    lo = (m - hi.astype(np.float64)).astype(ml_dtypes.bfloat16)
    return np.stack([hi, lo])


def trig(a, b):
    t = 2.0 * math.pi * ((np.asarray(a)[:, None] * np.asarray(b)[None, :]) % L) / L
    return np.cos(t), np.sin(t)


def complex_map(c, s, sign):
    m = np.zeros((2, 2) + c.shape)
    m[0, 0], m[1, 1] = c, c
    m[1, 0], m[0, 1] = -sign * s, sign * s
    return m


def first_matrix(sign, scale):
    c, s = trig(np.arange(L), np.arange(L))
    m = complex_map(c, s, sign) * scale
    return split_np(m.transpose(1, 3, 0, 2).reshape(2 * L, 2 * L))


def second_matrix(sign, scale, grouped):
    c, s = trig(np.arange(L), np.arange(L))
    m = complex_map(c, s, sign) * scale
    m = m.reshape(2, 2, L, 2, 2, 16)
    full = np.zeros((2, 2, L, 2, 2, 2, 2, 16))
    for pair in range(2):
        full[:, pair, :, :, :, pair] = m.transpose(0, 2, 3, 4, 1, 5)
    if not grouped:
        full = full.transpose(0, 1, 2, 3, 5, 6, 4, 7)
    return split_np(full.reshape(4 * L, 4 * L))


def out_x_matrix():
    c, s = trig(np.arange(L), np.arange(L))
    m = complex_map(c, s, 1.0) * (-1.0 / L)
    m = m.reshape(2, 2, 2, 2, 16, 16, 4)
    full = np.zeros((3, 16, 2, 4, 2, 2, 4, 2, 16))
    for b in range(3):
        full[b, :, :, :, :, :, b] = m.transpose(5, 1, 6, 2, 3, 0, 4)
    return split_np(full.reshape(3, 128, 512))


def out_y_matrix():
    c, s = trig(np.arange(L), np.arange(L))
    m = complex_map(c, s, 1.0) / L
    m = m.reshape(2, 2, 16, 4, L)
    full = np.zeros((4, 16, 2, 4, 4, 2, L))
    for k in range(4):
        full[:, :, :, k, k] = m.transpose(3, 2, 0, 1, 4)
    return split_np(full.reshape(512, 512))


def mm(a, b):
    return jnp.dot(a, b, preferred_element_type=F32)


def nt(a, b):
    return lax.dot_general(a, b, (((1,), (1,)), ((), ())), preferred_element_type=F32)


def halves(x):
    hi = x.astype(BF16)
    return hi, (x - hi.astype(F32)).astype(BF16)


def greet(axes):
    barrier = pltpu.get_barrier_semaphore()
    total = 0
    for axis, size in axes:
        me = lax.axis_index(axis)
        for i in range(1, size):
            pl.semaphore_signal(barrier, inc=1, device_id={axis: lax.rem(me + i, size)}, device_id_type=MESH)
        total += size - 1
    pl.semaphore_wait(barrier, total)


def exchange_green(green, vertex):
    def kernel(g_ref, v_ref, x_ref, vo_ref, gs, gr, vs, vr, own):
        greet([("bos", BOS)])
        me = lax.axis_index("bos")
        mine = [
            pltpu.make_async_copy(g_ref.at[:, me // 8, me % 8], x_ref.at[:, :, me], own.at[0]),
            pltpu.make_async_copy(v_ref, vo_ref.at[me], own.at[1]),
        ]
        copies = []
        for i in range(1, BOS):
            to = lax.rem(me + i, BOS)
            for k, (src, dst, ss, rs) in enumerate(
                (
                    (g_ref.at[:, to // 8, lax.rem(to, 8)], x_ref.at[:, :, me], gs, gr),
                    (v_ref, vo_ref.at[me], vs, vr),
                )
            ):
                copies.append(
                    pltpu.make_async_remote_copy(
                        src_ref=src,
                        dst_ref=dst,
                        send_sem=ss.at[i],
                        recv_sem=rs.at[i],
                        device_id={"bos": to},
                        device_id_type=MESH,
                    )
                )
        for c in copies:
            c.start()
        for c in mine:
            c.start()
        for c in mine:
            c.wait()
        for c in copies:
            c.wait()

    any_ = pl.BlockSpec(memory_space=pltpu.VMEM)
    return pl.pallas_call(
        kernel,
        out_shape=(
            jax.ShapeDtypeStruct((2, 9, BOS, 4, 128), BF16),
            jax.ShapeDtypeStruct((BOS, 8, 8), F32),
        ),
        in_specs=[any_, any_],
        out_specs=(any_, any_),
        scratch_shapes=[pltpu.SemaphoreType.DMA((BOS,))] * 4 + [pltpu.SemaphoreType.DMA((2,))],
        compiler_params=pltpu.CompilerParams(has_side_effects=True, collective_id=0),
        name="exchange_green",
    )(green, vertex)


def exchange_positions(sent):
    count = FER * BOS

    def kernel(s_ref, r_ref, ss, rs, own, seen):
        greet([("bos", BOS), ("fer", FER)])
        f, j = lax.axis_index("fer"), lax.axis_index("bos")
        me = j * FER + f
        row = count - 1 - ((j // 8) * 64 + f * 8 + lax.rem(j, 8))
        mine = pltpu.make_async_copy(s_ref.at[me], r_ref.at[row], own)
        mine.start()
        for i in range(1, FER):
            pl.semaphore_signal(seen, inc=1, device_id={"fer": lax.rem(f + i, FER)}, device_id_type=MESH)
        pl.semaphore_wait(seen, FER - 1)

        def send(i, carry):
            to = lax.rem(me + i, count)
            pltpu.make_async_remote_copy(
                src_ref=s_ref.at[to],
                dst_ref=r_ref.at[row],
                send_sem=ss,
                recv_sem=rs,
                device_id={"fer": lax.rem(to, FER), "bos": to // FER},
                device_id_type=MESH,
            ).start()
            return carry

        lax.fori_loop(1, count, send, 0)
        mine.wait()
        whole = pltpu.make_async_remote_copy(
            src_ref=s_ref.at[pl.ds(0, count - 1)],
            dst_ref=r_ref.at[pl.ds(0, count - 1)],
            send_sem=ss,
            recv_sem=rs,
            device_id={"fer": f, "bos": lax.rem(j + 1, BOS)},
            device_id_type=MESH,
        )
        whole.wait()

    any_ = pl.BlockSpec(memory_space=pltpu.VMEM)
    return pl.pallas_call(
        kernel,
        out_shape=jax.ShapeDtypeStruct((count, 16, 128), F32),
        in_specs=[any_],
        out_specs=any_,
        scratch_shapes=[pltpu.SemaphoreType.DMA] * 3 + [pltpu.SemaphoreType.REGULAR],
        compiler_params=pltpu.CompilerParams(has_side_effects=True, collective_id=1, vmem_limit_bytes=VMEM_LIMIT),
        name="exchange_positions",
    )(sent)


def exchange_axis(sent, axis, size, pick, out_shape, name):
    def kernel(s_ref, r_ref, ss, rs, own):
        greet([(axis, size)])
        me = lax.axis_index(axis)
        mine = pltpu.make_async_copy(pick(s_ref, me), r_ref.at[me], own)
        copies = []
        for i in range(1, size):
            to = lax.rem(me + i, size)
            copies.append(
                pltpu.make_async_remote_copy(
                    src_ref=pick(s_ref, to),
                    dst_ref=r_ref.at[me],
                    send_sem=ss.at[i],
                    recv_sem=rs.at[i],
                    device_id={axis: to},
                    device_id_type=MESH,
                )
            )
        for c in copies:
            c.start()
        mine.start()
        mine.wait()
        for c in copies:
            c.wait()

    any_ = pl.BlockSpec(memory_space=pltpu.VMEM)
    return pl.pallas_call(
        kernel,
        out_shape=jax.ShapeDtypeStruct(out_shape, F32),
        in_specs=[any_],
        out_specs=any_,
        scratch_shapes=[pltpu.SemaphoreType.DMA((size,))] * 2 + [pltpu.SemaphoreType.DMA],
        compiler_params=pltpu.CompilerParams(has_side_effects=True, collective_id=2 if axis == "fer" else 3),
        name=name,
    )(sent)


def to_positions(planes, weight, vertex_row, mats):
    def kernel(x_ref, w_ref, v_ref, g1, g2, w1, w2, s_ref):
        def both(x, m1, m2, row):
            z = nt(m1[0], x) + nt(m1[1], x)
            hi, lo = halves(jnp.concatenate([z[:L], z[L:]], axis=1))
            y = mm(hi, m2[0]) + mm(hi, m2[1]) + mm(lo, m2[0])
            for half in range(2):
                s_ref[:, half, row, :] = y[:, half * 128 : half * 128 + 128]

        for ac in range(9):
            both(jnp.concatenate([x_ref[0, ac], x_ref[1, ac]], axis=0), g1, g2, ac)
        for k in range(5):
            x = w_ref[0, 128 * k : 128 * k + 128] if k < 4 else w_ref[0, 512:576]
            if k == 4:
                x = jnp.concatenate([x, jnp.zeros((64, 128), BF16)], axis=0)
            both(x, w1, w2, 9 + k)
        s_ref[:, :, 14, :] = jnp.broadcast_to(v_ref[...].reshape(1, 1, 128), (L, 2, 128))
        s_ref[:, :, 15, :] = jnp.zeros((L, 2, 128), F32)

    vm = pl.BlockSpec(memory_space=pltpu.VMEM)
    return pl.pallas_call(
        kernel,
        out_shape=jax.ShapeDtypeStruct((L, 2, 16, 128), F32),
        in_specs=[vm] * 7,
        out_specs=vm,
        compiler_params=pltpu.CompilerParams(vmem_limit_bytes=VMEM_LIMIT),
        name="to_positions",
    )(planes, weight, vertex_row, *mats)


def contract(received, block_order, window_start):
    def kernel(bo, ws, r_ref, o_ref, gt, wk, wb, vert, h0, h1, rows):
        s = ws[0]
        lane = lax.broadcasted_iota(jnp.int32, (128, 128), 1)
        for ac in range(9):
            gt[ac] = r_ref[:, ac, :].T
        for j in range(BOS):
            base = (1 - j // 8) * 64 + (7 - j % 8)
            to = pl.multiple_of(8 * (15 - bo[j]), 8)
            for k in range(5):
                wk[k, pl.ds(to, 8), :] = r_ref[pl.ds(base, 8, stride=8), 9 + k, :]
        for rg in range(2):
            for c in range(3):
                t = jnp.zeros((128, 128), F32)
                for b in range(3):
                    k, odd = divmod(3 * c + b, 2)
                    by = (32 * b - 64 * rg - 32 * odd) % 128
                    piece = wk[k]
                    if by:
                        piece = pltpu.roll(piece, by, axis=1)
                    t = jnp.where(lane // 32 == b, piece, t)
                turned = jnp.where(
                    lane % 32 < 16, -pltpu.roll(t, 112, axis=1), pltpu.roll(t, 16, axis=1)
                )
                for ri, part in enumerate((t, turned)):
                    hi, lo = halves(part)
                    at = slice((2 * c + ri) * 128, (2 * c + ri) * 128 + 128)
                    wb[rg, at, 0:128] = hi
                    wb[rg, at, 128:256] = lo
        lane8 = lax.broadcasted_iota(jnp.int32, (8, 128), 1)
        raw = [r_ref[8 * (7 - o) : 8 * (7 - o) + 8, 14, :] for o in range(8)]
        turned = [jnp.zeros((8, 128), F32) for _ in range(8)]
        for j in range(BOS):
            by = lax.rem(8 * (j - bo[j]) + 128, 128)
            here = lane8 // 8 == 15 - bo[j]
            for o in range(8):
                turned[o] = jnp.where(here, pltpu.roll(raw[o], by, axis=1), turned[o])
        for o in range(8):
            vert[8 * o : 8 * o + 8, :] = turned[o]
        lane16 = lax.broadcasted_iota(jnp.int32, (16, 128), 1)

        def build(block, h_ref):
            for vi in range(8):
                by = s + (8 * block + vi)
                upper = lane16 >= 128 - by
                row = jnp.broadcast_to(vert[pl.ds(8 * block + vi, 1), :], (16, 128))
                for rg in range(2):
                    for a in range(3):
                        for cr in range(6):
                            ac, at = 3 * a + cr // 2, (cr % 2) * 32 + rg * 16
                            y = jnp.where(upper, gt[ac, 64 + at : 80 + at, :], gt[ac, at : at + 16, :])
                            hi, lo = halves(pltpu.roll(y, by, axis=1) * row)
                            to = (vi * 3 + a) * 16
                            h_ref[rg, to : to + 16, cr * 128 : cr * 128 + 128] = hi
                            h_ref[rg, 384 + to : 400 + to, cr * 128 : cr * 128 + 128] = lo

        def multiply(block, h_ref):
            for rg in range(2):
                acc = mm(h_ref[rg], wb[rg])
                acc = acc[:384] + acc[384:]
                rows[rg] = (acc[:, :128] + acc[:, 128:]).reshape(8, 48, 128)
                for a in range(3):
                    out = jnp.zeros((8, 128), F32)
                    for r16 in range(16):
                        out = jnp.where(lane8 % 16 == r16, rows[rg, :, a * 16 + r16, :], out)
                    o_ref[rg, a, pl.ds(8 * block, 8), :] = out

        slots = (h0, h1)
        build(0, h0)
        for block in range(8):
            if block < 7:
                build(block + 1, slots[(block + 1) % 2])
            multiply(block, slots[block % 2])

    vm = pl.BlockSpec(memory_space=pltpu.VMEM)
    sm = pl.BlockSpec(memory_space=pltpu.SMEM)
    return pl.pallas_call(
        kernel,
        out_shape=jax.ShapeDtypeStruct((2, 3, 64, 128), F32),
        in_specs=[sm, sm, vm],
        out_specs=vm,
        scratch_shapes=[
            pltpu.VMEM((9, 128, 128), F32),
            pltpu.VMEM((5, 128, 128), F32),
            pltpu.VMEM((2, 768, 256), BF16),
            pltpu.VMEM((64, 128), F32),
            pltpu.VMEM((2, 768, 768), BF16),
            pltpu.VMEM((2, 768, 768), BF16),
            pltpu.VMEM((2, 8, 48, 128), F32),
        ],
        compiler_params=pltpu.CompilerParams(vmem_limit_bytes=VMEM_LIMIT),
        name="contract",
    )(block_order, window_start, received)


def back_x(got, mat):
    def kernel(b_ref, m_ref, f_ref, lh, ll):
        lh[96:, :] = jnp.zeros((32, 512), BF16)
        ll[96:, :] = jnp.zeros((32, 512), BF16)
        for ryl in range(4):
            for half in range(2):
                for rg in range(2):
                    x = b_ref[2 * ryl + half, rg].reshape(24, 128)
                    hi, lo = halves(x)
                    at = (slice(24 * ryl, 24 * ryl + 24), slice((2 * half + rg) * 128, (2 * half + rg) * 128 + 128))
                    lh[at] = hi
                    ll[at] = lo
        for b in range(3):
            y = nt(m_ref[0, b], lh[...]) + nt(m_ref[0, b], ll[...]) + nt(m_ref[1, b], lh[...])
            f_ref[:, :, b * 128 : b * 128 + 128] = y.reshape(16, 8, 128)

    vm = pl.BlockSpec(memory_space=pltpu.VMEM)
    return pl.pallas_call(
        kernel,
        out_shape=jax.ShapeDtypeStruct((BOS, 8, 384), F32),
        in_specs=[vm, vm],
        out_specs=vm,
        scratch_shapes=[pltpu.VMEM((128, 512), BF16)] * 2,
        name="back_x",
    )(got, mat)


def back_y(got, mat):
    def kernel(e_ref, m_ref, o_ref, lh, ll):
        for b in range(3):
            t = e_ref[:, :, b * 128 : b * 128 + 128].reshape(128, 128).T
            hi, lo = halves(t)
            for ryl in range(4):
                at = (slice(24 * b, 24 * b + 24), slice(128 * ryl, 128 * ryl + 128))
                lh[at] = hi[24 * ryl : 24 * ryl + 24]
                ll[at] = lo[24 * ryl : 24 * ryl + 24]
        y = mm(lh[...], m_ref[0]) + mm(ll[...], m_ref[0]) + mm(lh[...], m_ref[1])
        for b in range(3):
            for a in range(3):
                for k in range(4):
                    o_ref[k, 3 * a + b] = y[24 * b + 8 * a : 24 * b + 8 * a + 8, 128 * k : 128 * k + 128]

    vm = pl.BlockSpec(memory_space=pltpu.VMEM)
    return pl.pallas_call(
        kernel,
        out_shape=jax.ShapeDtypeStruct((4, 9, 8, 128), F32),
        in_specs=[vm, vm],
        out_specs=vm,
        scratch_shapes=[pltpu.VMEM((72, 512), BF16)] * 2,
        name="back_y",
    )(got, mat)


def body(green, bos_weight, vertex, block_order, window_start):
    f, j = lax.axis_index("fer"), lax.axis_index("bos")
    planes, rows = exchange_green(green.reshape(2, 2, 8, 9, 4, 128), vertex)
    rows = rows.transpose(1, 0, 2).reshape(8, 128)[:, ::-1]
    row = lax.dynamic_slice_in_dim(rows, 7 - j % 8, 1, 0)
    weight = lax.dynamic_slice_in_dim(bos_weight, f, 1, 0).reshape(1, 576, 128)
    mats = [
        jnp.asarray(first_matrix(-1.0, 1.0)),
        jnp.asarray(second_matrix(-1.0, 1.0, False)),
        jnp.asarray(first_matrix(1.0, 1.0 / L)),
        jnp.asarray(second_matrix(1.0, 1.0 / L, True)),
    ]
    sent = to_positions(planes.reshape(2, 9, L, 128), weight, row, mats)
    got = exchange_positions(sent.reshape(128, 16, 128))
    part = contract(got, block_order, window_start)
    octets = exchange_axis(
        part, "fer", FER, lambda ref, to: ref.at[:, :, pl.ds(pl.multiple_of(8 * to, 8), 8), :], (FER, 2, 3, 8, 128), "exchange_octets"
    )
    quads = back_x(octets, jnp.asarray(out_x_matrix()))
    last = exchange_axis(quads, "bos", BOS, lambda ref, to: ref.at[to], (BOS, 8, 384), "exchange_rows")
    return back_y(last, jnp.asarray(out_y_matrix())).transpose(0, 2, 1, 3)


def solution(mesh):
    return jax.shard_map(
        body,
        mesh=mesh,
        in_specs=(
            P(None, "fer", None, "bos", None),
            P("bos", None, None, None),
            P("fer", "bos"),
            P(),
            P(),
        ),
        out_specs=P("bos", "fer", None, None),
        check_vma=False,
    )
```

```python
import functools
import math

import jax
import jax.numpy as jnp
import ml_dtypes
import numpy as np
from jax import lax
from jax.experimental import pallas as pl
from jax.experimental.pallas import tpu as pltpu
from jax.sharding import PartitionSpec as P

MESH = pl.DeviceIdType.MESH
BF16 = jnp.bfloat16
F32 = jnp.float32
L = 64
FER = 8
BOS = 16
VMEM_LIMIT = 56 * 1024 * 1024


def split_np(m):
    hi = m.astype(ml_dtypes.bfloat16)
    lo = (m - hi.astype(np.float64)).astype(ml_dtypes.bfloat16)
    return np.stack([hi, lo])


def trig(a, b):
    t = 2.0 * math.pi * ((np.asarray(a)[:, None] * np.asarray(b)[None, :]) % L) / L
    return np.cos(t), np.sin(t)


def complex_map(c, s, sign):
    m = np.zeros((2, 2) + c.shape)
    m[0, 0], m[1, 1] = c, c
    m[1, 0], m[0, 1] = -sign * s, sign * s
    return m


def first_matrix(sign, scale):
    c, s = trig(np.arange(L), np.arange(L))
    m = complex_map(c, s, sign) * scale
    return split_np(m.transpose(1, 3, 0, 2).reshape(2 * L, 2 * L))


def second_matrix(sign, scale, grouped):
    c, s = trig(np.arange(L), np.arange(L))
    m = complex_map(c, s, sign) * scale
    m = m.reshape(2, 2, L, 2, 2, 16)
    full = np.zeros((2, 2, L, 2, 2, 2, 2, 16))
    for pair in range(2):
        full[:, pair, :, :, :, pair] = m.transpose(0, 2, 3, 4, 1, 5)
    if not grouped:
        full = full.transpose(0, 1, 2, 3, 5, 6, 4, 7)
    return split_np(full.reshape(4 * L, 4 * L))


def out_x_matrix():
    c, s = trig(np.arange(L), np.arange(L))
    m = complex_map(c, s, 1.0) * (-1.0 / L)
    m = m.reshape(2, 2, 2, 2, 16, 16, 4)
    full = np.zeros((3, 16, 2, 4, 2, 2, 4, 2, 16))
    for b in range(3):
        full[b, :, :, :, :, :, b] = m.transpose(5, 1, 6, 2, 3, 0, 4)
    return split_np(full.reshape(3, 128, 512))


def out_y_matrix():
    c, s = trig(np.arange(L), np.arange(L))
    m = complex_map(c, s, 1.0) / L
    m = m.reshape(2, 2, 16, 4, L)
    full = np.zeros((4, 16, 2, 4, 4, 2, L))
    for k in range(4):
        full[:, :, :, k, k] = m.transpose(3, 2, 0, 1, 4)
    return split_np(full.reshape(512, 512))


def mm(a, b):
    return jnp.dot(a, b, preferred_element_type=F32)


def nt(a, b):
    return lax.dot_general(a, b, (((1,), (1,)), ((), ())), preferred_element_type=F32)


def halves(x):
    hi = x.astype(BF16)
    return hi, (x - hi.astype(F32)).astype(BF16)


def ring(axis, size, start):
    me = lax.axis_index(axis)
    copies = []
    for i in range(1, size):
        to = lax.rem(me + i, size)
        copies.append(
            pltpu.make_async_remote_copy(device_id={axis: to}, device_id_type=MESH, **start(to, i))
        )
    return copies


def transform(x, m1, m2, s_ref, row):
    z = nt(m1[0], x) + nt(m1[1], x)
    hi, lo = halves(jnp.concatenate([z[:L], z[L:]], axis=1))
    y = mm(hi, m2[0]) + mm(hi, m2[1]) + mm(lo, m2[0])
    for half in range(2):
        s_ref[:, half, row, :] = y[:, half * 128 : half * 128 + 128]


def whole_kernel(
    bo, ws, green, weight, vertex, g1h, g2h, w1h, w2h, mxh, myh, out,
    g1, g2, w1, w2, mx, my, planes, vsend, vgot, vsum, sg, sw, rg_in, rw_in,
    gt, wk, wb, vert, h0, h1, rows, octets, b_in, lh, ll, quads, e_in, yh, yl,
    csem, green_s, green_r, vert_s, vert_r, pos_s, pos_r, own, oct_s, oct_r, quad_s, quad_r, seen,
):
    f, j = lax.axis_index("fer"), lax.axis_index("bos")
    me = j * FER + f
    place = (j // 8) * 64 + f * 8 + lax.rem(j, 8)
    count = FER * BOS

    barrier = pltpu.get_barrier_semaphore()
    for axis, size, mine in (("bos", BOS, j), ("fer", FER, f)):
        for i in range(1, size):
            pl.semaphore_signal(
                barrier, inc=1, device_id={axis: lax.rem(mine + i, size)}, device_id_type=MESH
            )
    loads = [
        pltpu.make_async_copy(a, b, csem.at[i])
        for i, (a, b) in enumerate(
            ((w1h, w1), (w2h, w2), (g1h, g1), (g2h, g2), (mxh, mx), (myh, my))
        )
    ]
    for c in loads:
        c.start()

    loads[0].wait()
    loads[1].wait()
    for k in range(5):
        if k < 4:
            x = weight[f, 128 * k : 128 * k + 128]
        else:
            x = jnp.concatenate([weight[f, 512:576], jnp.zeros((64, 128), BF16)], axis=0)
        transform(x, w1, w2, sw, k)
    lane8 = lax.broadcasted_iota(jnp.int32, (8, 128), 1)
    spread = jnp.concatenate([vertex[...]] * BOS, axis=1)
    vsend[...] = jnp.where(lane8 // 8 == bo[j], spread, 0.0)

    pl.semaphore_wait(barrier, BOS + FER - 2)
    for i in range(1, FER):
        pl.semaphore_signal(seen, inc=1, device_id={"fer": lax.rem(f + i, FER)}, device_id_type=MESH)

    near = ring(
        "bos", BOS,
        lambda to, i: dict(
            src_ref=green.at[:, to // 8, lax.rem(to, 8)], dst_ref=planes.at[:, :, j],
            send_sem=green_s.at[i], recv_sem=green_r.at[i],
        ),
    )
    near += ring(
        "bos", BOS,
        lambda to, i: dict(
            src_ref=vsend, dst_ref=vgot.at[j], send_sem=vert_s.at[i], recv_sem=vert_r.at[i]
        ),
    )
    for c in near:
        c.start()
    kept = pltpu.make_async_copy(green.at[:, j // 8, lax.rem(j, 8)], planes.at[:, :, j], own.at[0])
    kept.start()
    vgot[j] = vsend[...]

    pl.semaphore_wait(seen, FER - 1)

    def everywhere(src, dst, which):
        mine = pltpu.make_async_copy(src.at[me // 2, lax.rem(me, 2)], dst.at[place], own.at[1 + which])
        mine.start()

        def send(i, carry):
            to = lax.rem(me + i, count)
            pltpu.make_async_remote_copy(
                src_ref=src.at[to // 2, lax.rem(to, 2)],
                dst_ref=dst.at[place],
                send_sem=pos_s.at[which],
                recv_sem=pos_r.at[which],
                device_id={"fer": lax.rem(to, FER), "bos": to // FER},
                device_id_type=MESH,
            ).start()
            return carry

        lax.fori_loop(1, count, send, 0)
        return mine

    def arrived(dst, which):
        part = dst.at[pl.ds(0, count - 1)]
        pltpu.make_async_remote_copy(
            src_ref=part, dst_ref=part, send_sem=pos_s.at[which], recv_sem=pos_r.at[which],
            device_id={"bos": lax.rem(j + 1, BOS)}, device_id_type=MESH,
        ).wait()

    mine_w = everywhere(sw, rw_in, 0)

    kept.wait()
    for c in near:
        c.wait()
    total = vgot[0]
    for i in range(1, BOS):
        total = total + vgot[i]
    vsum[...] = total
    sg[:, :, 9, :] = jnp.broadcast_to(
        vsum[pl.ds(lax.rem(j, 8), 1), :].reshape(1, 1, 128), (L, 2, 128)
    )
    loads[2].wait()
    loads[3].wait()
    for ac in range(9):
        x = jnp.concatenate([planes[n2, ac].reshape(L, 128) for n2 in range(2)], axis=0)
        transform(x, g1, g2, sg, ac)
    mine_g = everywhere(sg, rg_in, 1)

    mine_w.wait()
    arrived(rw_in, 0)
    lane = lax.broadcasted_iota(jnp.int32, (128, 128), 1)
    sub = lax.broadcasted_iota(jnp.int32, (128, 128), 0)
    target = jnp.zeros((8, 128), jnp.int32)
    owner = (lane8 // 64) * 8 + lane8 % 8
    for i in range(BOS):
        target = jnp.where(owner == i, bo[i] * 8, target)
    target = target + lane8 // 8 % 8
    order = jnp.where(sub == jnp.concatenate([target] * 16, axis=0), 1.0, 0.0).astype(BF16)
    for k in range(5):
        hi, lo = halves(rw_in[:, k, :])
        wk[k] = mm(order, hi) + mm(order, lo)
    for rg in range(2):
        for c in range(3):
            t = jnp.zeros((128, 128), F32)
            for b in range(3):
                k, odd = divmod(3 * c + b, 2)
                by = (32 * b - 64 * rg - 32 * odd) % 128
                piece = pltpu.roll(wk[k], by, axis=1) if by else wk[k]
                t = jnp.where(lane // 32 == b, piece, t)
            turned = jnp.where(lane % 32 < 16, -pltpu.roll(t, 112, axis=1), pltpu.roll(t, 16, axis=1))
            for ri, part in enumerate((t, turned)):
                hi, lo = halves(part)
                at = slice((2 * c + ri) * 128, (2 * c + ri) * 128 + 128)
                wb[rg, at, 0:128] = hi
                wb[rg, at, 128:256] = lo

    mine_g.wait()
    arrived(rg_in, 1)
    for ac in range(9):
        gt[ac] = rg_in[:, ac, :].T
    vert[...] = rg_in[0:64, 9, :]

    s = ws[0]
    lane16 = lax.broadcasted_iota(jnp.int32, (16, 128), 1)

    def octet(t):
        return lax.rem(f + 1 + t, FER)

    def build(t, h_ref):
        base = 8 * octet(t)
        for vi in range(8):
            by = s + base + vi
            upper = lane16 >= by
            back = lax.rem(128 - by, 128)
            row = jnp.broadcast_to(vert[pl.ds(base + vi, 1), :], (16, 128))
            for rg in range(2):
                for a in range(3):
                    for cr in range(6):
                        ac, at = 3 * a + cr // 2, (cr % 2) * 32 + rg * 16
                        y = jnp.where(upper, gt[ac, at : at + 16, :], gt[ac, 64 + at : 80 + at, :])
                        hi, lo = halves(pltpu.roll(y, back, axis=1) * row)
                        to = (vi * 3 + a) * 16
                        h_ref[rg, to : to + 16, cr * 128 : cr * 128 + 128] = hi
                        h_ref[rg, 384 + to : 400 + to, cr * 128 : cr * 128 + 128] = lo

    def multiply(t, h_ref):
        for rg in range(2):
            acc = mm(h_ref[rg], wb[rg])
            acc = acc[:384] + acc[384:]
            rows[rg] = (acc[:, :128] + acc[:, 128:]).reshape(8, 48, 128)
            for a in range(3):
                o = jnp.zeros((8, 128), F32)
                for r16 in range(16):
                    o = jnp.where(lane8 % 16 == r16, rows[rg, :, a * 16 + r16, :], o)
                octets[t, rg, a] = o

    def pass_on(t):
        return pltpu.make_async_remote_copy(
            src_ref=octets.at[t], dst_ref=b_in.at[f],
            send_sem=oct_s.at[t], recv_sem=oct_r.at[t],
            device_id={"fer": octet(t)}, device_id_type=MESH,
        )

    build(0, h0)

    def pair(t, carry):
        build(2 * t + 1, h1)
        multiply(2 * t, h0)
        pass_on(2 * t).start()
        build(jnp.minimum(2 * t + 2, 7), h0)
        multiply(2 * t + 1, h1)

        @pl.when(t < 3)
        def _():
            pass_on(2 * t + 1).start()

        return carry

    lax.fori_loop(0, 4, pair, 0)
    b_in[f] = octets[7]
    for t in range(7):
        pass_on(t).wait()

    lh[96:, :] = jnp.zeros((32, 512), BF16)
    ll[96:, :] = jnp.zeros((32, 512), BF16)
    for ryl in range(4):
        for half in range(2):
            for rg in range(2):
                hi, lo = halves(b_in[2 * ryl + half, rg].reshape(24, 128))
                at = (
                    slice(24 * ryl, 24 * ryl + 24),
                    slice((2 * half + rg) * 128, (2 * half + rg) * 128 + 128),
                )
                lh[at] = hi
                ll[at] = lo
    loads[4].wait()
    for b in range(3):
        y = nt(mx[0, b], lh[...]) + nt(mx[0, b], ll[...]) + nt(mx[1, b], lh[...])
        quads[:, :, b * 128 : b * 128 + 128] = y.reshape(BOS, 8, 128)
    last = ring(
        "bos", BOS,
        lambda to, i: dict(
            src_ref=quads.at[to], dst_ref=e_in.at[j], send_sem=quad_s.at[i], recv_sem=quad_r.at[i]
        ),
    )
    for c in last:
        c.start()
    e_in[j] = quads[j]
    loads[5].wait()
    for c in last:
        c.wait()

    for b in range(3):
        hi, lo = halves(e_in[:, :, b * 128 : b * 128 + 128].reshape(128, 128).T)
        for ryl in range(4):
            at = (slice(24 * b, 24 * b + 24), slice(128 * ryl, 128 * ryl + 128))
            yh[at] = hi[24 * ryl : 24 * ryl + 24]
            yl[at] = lo[24 * ryl : 24 * ryl + 24]
    y = mm(yh[...], my[0]) + mm(yl[...], my[0]) + mm(yh[...], my[1])
    for b in range(3):
        for a in range(3):
            for k in range(4):
                out[k, 3 * a + b] = y[24 * b + 8 * a : 24 * b + 8 * a + 8, 128 * k : 128 * k + 128]


def body(green, bos_weight, vertex, block_order, window_start):
    mats = [
        first_matrix(-1.0, 1.0),
        second_matrix(-1.0, 1.0, False),
        first_matrix(1.0, 1.0 / L),
        second_matrix(1.0, 1.0 / L, True),
        out_x_matrix(),
        out_y_matrix(),
    ]
    vm = pl.BlockSpec(memory_space=pltpu.VMEM)
    sm = pl.BlockSpec(memory_space=pltpu.SMEM)
    hbm = pl.BlockSpec(memory_space=pl.ANY)
    dma = pltpu.SemaphoreType.DMA
    out = pl.pallas_call(
        whole_kernel,
        out_shape=jax.ShapeDtypeStruct((4, 9, 8, 128), F32),
        in_specs=[sm, sm, vm, vm, vm] + [hbm] * 6,
        out_specs=vm,
        scratch_shapes=[pltpu.VMEM(m.shape, BF16) for m in mats]
        + [
            pltpu.VMEM((2, 9, BOS, 4, 128), BF16),
            pltpu.VMEM((8, 128), F32),
            pltpu.VMEM((BOS, 8, 128), F32),
            pltpu.VMEM((8, 128), F32),
            pltpu.VMEM((L, 2, 10, 128), F32),
            pltpu.VMEM((L, 2, 5, 128), F32),
            pltpu.VMEM((128, 10, 128), F32),
            pltpu.VMEM((128, 5, 128), F32),
            pltpu.VMEM((9, 128, 128), F32),
            pltpu.VMEM((5, 128, 128), F32),
            pltpu.VMEM((2, 768, 256), BF16),
            pltpu.VMEM((64, 128), F32),
            pltpu.VMEM((2, 768, 768), BF16),
            pltpu.VMEM((2, 768, 768), BF16),
            pltpu.VMEM((2, 8, 48, 128), F32),
            pltpu.VMEM((FER, 2, 3, 8, 128), F32),
            pltpu.VMEM((FER, 2, 3, 8, 128), F32),
            pltpu.VMEM((128, 512), BF16),
            pltpu.VMEM((128, 512), BF16),
            pltpu.VMEM((BOS, 8, 384), F32),
            pltpu.VMEM((BOS, 8, 384), F32),
            pltpu.VMEM((72, 512), BF16),
            pltpu.VMEM((72, 512), BF16),
            dma((6,)), dma((BOS,)), dma((BOS,)), dma((BOS,)), dma((BOS,)), dma((2,)), dma((2,)), dma((3,)),
            dma((FER,)), dma((FER,)), dma((BOS,)), dma((BOS,)), pltpu.SemaphoreType.REGULAR,
        ],
        compiler_params=pltpu.CompilerParams(
            has_side_effects=True, collective_id=0, vmem_limit_bytes=VMEM_LIMIT
        ),
        name="dual_self_energy",
    )(
        block_order,
        window_start,
        green.reshape(2, 2, 8, 9, 4, 128),
        bos_weight.reshape(8, 576, 128),
        vertex,
        *[jnp.asarray(m) for m in (mats[0], mats[1], mats[2], mats[3], mats[4], mats[5])],
    )
    return out.transpose(0, 2, 1, 3)


def solution(mesh):
    return jax.shard_map(
        body,
        mesh=mesh,
        in_specs=(
            P(None, "fer", None, "bos", None),
            P("bos", None, None, None),
            P("fer", "bos"),
            P(),
            P(),
        ),
        out_specs=P("bos", "fer", None, None),
        check_vma=False,
    )
```

```python
import functools
import math

import jax
import jax.numpy as jnp
import ml_dtypes
import numpy as np
from jax import lax
from jax.experimental import pallas as pl
from jax.experimental.pallas import tpu as pltpu
from jax.sharding import PartitionSpec as P

MESH = pl.DeviceIdType.MESH
BF16 = jnp.bfloat16
F32 = jnp.float32
L = 64
FER = 8
BOS = 16
VMEM_LIMIT = 56 * 1024 * 1024


def split_np(m):
    hi = m.astype(ml_dtypes.bfloat16)
    lo = (m - hi.astype(np.float64)).astype(ml_dtypes.bfloat16)
    return np.stack([hi, lo])


def trig(a, b):
    t = 2.0 * math.pi * ((np.asarray(a)[:, None] * np.asarray(b)[None, :]) % L) / L
    return np.cos(t), np.sin(t)


def complex_map(c, s, sign):
    m = np.zeros((2, 2) + c.shape)
    m[0, 0], m[1, 1] = c, c
    m[1, 0], m[0, 1] = -sign * s, sign * s
    return m


def first_matrix(sign, scale):
    c, s = trig(np.arange(L), np.arange(L))
    m = complex_map(c, s, sign) * scale
    return split_np(m.transpose(1, 3, 0, 2).reshape(2 * L, 2 * L))


def second_matrix(sign, scale, grouped):
    c, s = trig(np.arange(L), np.arange(L))
    m = complex_map(c, s, sign) * scale
    m = m.reshape(2, 2, L, 2, 2, 16)
    full = np.zeros((2, 2, L, 2, 2, 2, 2, 16))
    for pair in range(2):
        full[:, pair, :, :, :, pair] = m.transpose(0, 2, 3, 4, 1, 5)
    if not grouped:
        full = full.transpose(0, 1, 2, 3, 5, 6, 4, 7)
    return split_np(full.reshape(4 * L, 4 * L))


def out_x_matrix():
    c, s = trig(np.arange(L), np.arange(L))
    m = complex_map(c, s, 1.0) * (-1.0 / L)
    m = m.reshape(2, 2, 2, 2, 16, 16, 4)
    full = np.zeros((3, 16, 2, 4, 2, 2, 4, 2, 16))
    for b in range(3):
        full[b, :, :, :, :, :, b] = m.transpose(5, 1, 6, 2, 3, 0, 4)
    return split_np(full.reshape(3, 128, 512))


def out_y_matrix():
    c, s = trig(np.arange(L), np.arange(L))
    m = complex_map(c, s, 1.0) / L
    m = m.reshape(2, 2, 16, 4, L)
    full = np.zeros((4, 16, 2, 4, 4, 2, L))
    for k in range(4):
        full[:, :, :, k, k] = m.transpose(3, 2, 0, 1, 4)
    return split_np(full.reshape(512, 512))


def mm(a, b):
    return jnp.dot(a, b, preferred_element_type=F32)


def nt(a, b):
    return lax.dot_general(a, b, (((1,), (1,)), ((), ())), preferred_element_type=F32)


def halves(x):
    hi = x.astype(BF16)
    return hi, (x - hi.astype(F32)).astype(BF16)


def hops(offset):
    return sum(min(d, 4 - d) for d in offset[:3]) + 0.5 * offset[3]


FAR_FIRST = sorted(
    [(z, y, x, c) for z in range(4) for y in range(4) for x in range(4) for c in range(2)][1:],
    key=hops,
    reverse=True,
)


def ring(axis, size, start):
    me = lax.axis_index(axis)
    copies = []
    for i in range(1, size):
        to = lax.rem(me + i, size)
        copies.append(
            pltpu.make_async_remote_copy(device_id={axis: to}, device_id_type=MESH, **start(to, i))
        )
    return copies


def transform(x, m1, m2, s_ref, row):
    z = nt(m1[0], x) + nt(m1[1], x)
    hi, lo = halves(jnp.concatenate([z[:L], z[L:]], axis=1))
    y = mm(hi, m2[0]) + mm(hi, m2[1]) + mm(lo, m2[0])
    for half in range(2):
        s_ref[:, half, row, :] = y[:, half * 128 : half * 128 + 128]


def whole_kernel(
    bo, ws, green, weight, vertex, g1h, g2h, w1h, w2h, mxh, myh, out,
    g1, g2, w1, w2, mx, my, planes, vsend, vgot, vsum, sa, sb, sw, ra_in, rb_in, rw_in,
    gt, wk, wb, vert, h0, h1, rows, octets, b_in, lh, ll, quads, e_in, yh, yl,
    csem, green_s, green_r, vert_s, vert_r, pos_s, pos_r, own, oct_s, oct_r, quad_s, quad_r, seen,
):
    f, j = lax.axis_index("fer"), lax.axis_index("bos")
    me = j * FER + f
    place = (j // 8) * 64 + f * 8 + lax.rem(j, 8)
    count = FER * BOS

    barrier = pltpu.get_barrier_semaphore()
    for axis, size, mine in (("bos", BOS, j), ("fer", FER, f)):
        for i in range(1, size):
            pl.semaphore_signal(
                barrier, inc=1, device_id={axis: lax.rem(mine + i, size)}, device_id_type=MESH
            )
    loads = [
        pltpu.make_async_copy(a, b, csem.at[i])
        for i, (a, b) in enumerate(
            ((w1h, w1), (w2h, w2), (g1h, g1), (g2h, g2), (mxh, mx), (myh, my))
        )
    ]
    for c in loads:
        c.start()

    loads[0].wait()
    loads[1].wait()
    for k in range(5):
        if k < 4:
            x = weight[f, 128 * k : 128 * k + 128]
        else:
            x = jnp.concatenate([weight[f, 512:576], jnp.zeros((64, 128), BF16)], axis=0)
        transform(x, w1, w2, sw, k)
    lane8 = lax.broadcasted_iota(jnp.int32, (8, 128), 1)
    spread = jnp.concatenate([vertex[...]] * BOS, axis=1)
    vsend[...] = jnp.where(lane8 // 8 == bo[j], spread, 0.0)

    pl.semaphore_wait(barrier, BOS + FER - 2)
    for i in range(1, FER):
        pl.semaphore_signal(seen, inc=1, device_id={"fer": lax.rem(f + i, FER)}, device_id_type=MESH)

    parts = (pl.ds(0, 5), pl.ds(5, 4))
    near = [
        ring(
            "bos", BOS,
            lambda to, i, h=h: dict(
                src_ref=green.at[:, to // 8, lax.rem(to, 8), parts[h]],
                dst_ref=planes.at[:, parts[h], j],
                send_sem=green_s.at[h, i], recv_sem=green_r.at[h, i],
            ),
        )
        for h in range(2)
    ]
    near[1] += ring(
        "bos", BOS,
        lambda to, i: dict(
            src_ref=vsend, dst_ref=vgot.at[j], send_sem=vert_s.at[i], recv_sem=vert_r.at[i]
        ),
    )
    for c in near[0] + near[1]:
        c.start()
    kept = pltpu.make_async_copy(green.at[:, j // 8, lax.rem(j, 8)], planes.at[:, :, j], own.at[0])
    kept.start()
    vgot[j] = vsend[...]

    pl.semaphore_wait(seen, FER - 1)

    def everywhere(src, dst, which):
        mine = pltpu.make_async_copy(src.at[me // 2, lax.rem(me, 2)], dst.at[place], own.at[1 + which])
        mine.start()

        for dz, dy, dx, dc in FAR_FIRST:
            x = lax.rem(lax.rem(j // 2, 4) + dx, 4)
            y = lax.rem(lax.rem(f, 2) * 2 + j // 8 + dy, 4)
            z = lax.rem(f // 2 + dz, 4)
            fi = z * 2 + y // 2
            ji = lax.rem(y, 2) * 8 + x * 2 + lax.rem(lax.rem(j, 2) + dc, 2)
            pltpu.make_async_remote_copy(
                src_ref=src.at[ji * 4 + fi // 2, lax.rem(fi, 2)],
                dst_ref=dst.at[place],
                send_sem=pos_s.at[which],
                recv_sem=pos_r.at[which],
                device_id={"fer": fi, "bos": ji},
                device_id_type=MESH,
            ).start()
        return mine

    def arrived(dst, which):
        part = dst.at[pl.ds(0, count - 1)]
        pltpu.make_async_remote_copy(
            src_ref=part, dst_ref=part, send_sem=pos_s.at[which], recv_sem=pos_r.at[which],
            device_id={"bos": lax.rem(j + 1, BOS)}, device_id_type=MESH,
        ).wait()

    mine_w = everywhere(sw, rw_in, 0)

    kept.wait()
    loads[2].wait()
    loads[3].wait()

    def planes_of(ac):
        return jnp.concatenate([planes[n2, ac].reshape(L, 128) for n2 in range(2)], axis=0)

    for c in near[0]:
        c.wait()
    for ac in range(5):
        transform(planes_of(ac), g1, g2, sa, ac)
    mine_a = everywhere(sa, ra_in, 1)
    for c in near[1]:
        c.wait()
    total = vgot[0]
    for i in range(1, BOS):
        total = total + vgot[i]
    vsum[...] = total
    sb[:, :, 4, :] = jnp.broadcast_to(
        vsum[pl.ds(lax.rem(j, 8), 1), :].reshape(1, 1, 128), (L, 2, 128)
    )
    for ac in range(5, 9):
        transform(planes_of(ac), g1, g2, sb, ac - 5)
    mine_b = everywhere(sb, rb_in, 2)

    mine_w.wait()
    arrived(rw_in, 0)
    lane = lax.broadcasted_iota(jnp.int32, (128, 128), 1)
    sub = lax.broadcasted_iota(jnp.int32, (128, 128), 0)
    target = jnp.zeros((8, 128), jnp.int32)
    owner = (lane8 // 64) * 8 + lane8 % 8
    for i in range(BOS):
        target = jnp.where(owner == i, bo[i] * 8, target)
    target = target + lane8 // 8 % 8
    order = jnp.where(sub == jnp.concatenate([target] * 16, axis=0), 1.0, 0.0).astype(BF16)
    for k in range(5):
        hi, lo = halves(rw_in[:, k, :])
        wk[k] = mm(order, hi) + mm(order, lo)
    for rg in range(2):
        for c in range(3):
            t = jnp.zeros((128, 128), F32)
            for b in range(3):
                k, odd = divmod(3 * c + b, 2)
                by = (32 * b - 64 * rg - 32 * odd) % 128
                piece = pltpu.roll(wk[k], by, axis=1) if by else wk[k]
                t = jnp.where(lane // 32 == b, piece, t)
            turned = jnp.where(lane % 32 < 16, -pltpu.roll(t, 112, axis=1), pltpu.roll(t, 16, axis=1))
            for ri, part in enumerate((t, turned)):
                hi, lo = halves(part)
                at = slice((2 * c + ri) * 128, (2 * c + ri) * 128 + 128)
                wb[rg, at, 0:128] = hi
                wb[rg, at, 128:256] = lo

    mine_a.wait()
    arrived(ra_in, 1)
    for ac in range(5):
        gt[ac] = ra_in[:, ac, :].T
    mine_b.wait()
    arrived(rb_in, 2)
    for ac in range(5, 9):
        gt[ac] = rb_in[:, ac - 5, :].T
    vert[...] = rb_in[0:64, 4, :]

    s = ws[0]
    lane16 = lax.broadcasted_iota(jnp.int32, (16, 128), 1)

    def octet(t):
        u = lax.rem(t, 4)
        dz = jnp.where(u == 3, 0, jnp.where(u == 2, 3, 2 - u))
        return lax.rem(f // 2 + dz, 4) * 2 + lax.rem(f + 1 + t // 4, 2)

    def build(t, h_ref):
        base = 8 * octet(t)
        for vi in range(8):
            by = s + base + vi
            upper = lane16 >= by
            back = lax.rem(128 - by, 128)
            row = jnp.broadcast_to(vert[pl.ds(base + vi, 1), :], (16, 128))
            for rg in range(2):
                for a in range(3):
                    for cr in range(6):
                        ac, at = 3 * a + cr // 2, (cr % 2) * 32 + rg * 16
                        y = jnp.where(upper, gt[ac, at : at + 16, :], gt[ac, 64 + at : 80 + at, :])
                        hi, lo = halves(pltpu.roll(y, back, axis=1) * row)
                        to = (vi * 3 + a) * 16
                        h_ref[rg, to : to + 16, cr * 128 : cr * 128 + 128] = hi
                        h_ref[rg, 384 + to : 400 + to, cr * 128 : cr * 128 + 128] = lo

    def multiply(t, h_ref):
        for rg in range(2):
            acc = mm(h_ref[rg], wb[rg])
            acc = acc[:384] + acc[384:]
            rows[rg] = (acc[:, :128] + acc[:, 128:]).reshape(8, 48, 128)
            for a in range(3):
                o = jnp.zeros((8, 128), F32)
                for r16 in range(16):
                    o = jnp.where(lane8 % 16 == r16, rows[rg, :, a * 16 + r16, :], o)
                octets[t, rg, a] = o

    def pass_on(t):
        return pltpu.make_async_remote_copy(
            src_ref=octets.at[t], dst_ref=b_in.at[f],
            send_sem=oct_s.at[t], recv_sem=oct_r.at[t],
            device_id={"fer": octet(t)}, device_id_type=MESH,
        )

    build(0, h0)

    def pair(t, carry):
        build(2 * t + 1, h1)
        multiply(2 * t, h0)
        pass_on(2 * t).start()
        build(jnp.minimum(2 * t + 2, 7), h0)
        multiply(2 * t + 1, h1)

        @pl.when(t < 3)
        def _():
            pass_on(2 * t + 1).start()

        return carry

    lax.fori_loop(0, 4, pair, 0)
    b_in[f] = octets[7]
    for t in range(7):
        pass_on(t).wait()

    lh[96:, :] = jnp.zeros((32, 512), BF16)
    ll[96:, :] = jnp.zeros((32, 512), BF16)
    for ryl in range(4):
        for half in range(2):
            for rg in range(2):
                hi, lo = halves(b_in[2 * ryl + half, rg].reshape(24, 128))
                at = (
                    slice(24 * ryl, 24 * ryl + 24),
                    slice((2 * half + rg) * 128, (2 * half + rg) * 128 + 128),
                )
                lh[at] = hi
                ll[at] = lo
    loads[4].wait()
    for b in range(3):
        y = nt(mx[0, b], lh[...]) + nt(mx[0, b], ll[...]) + nt(mx[1, b], lh[...])
        quads[:, :, b * 128 : b * 128 + 128] = y.reshape(BOS, 8, 128)
    last = ring(
        "bos", BOS,
        lambda to, i: dict(
            src_ref=quads.at[to], dst_ref=e_in.at[j], send_sem=quad_s.at[i], recv_sem=quad_r.at[i]
        ),
    )
    for c in last:
        c.start()
    e_in[j] = quads[j]
    loads[5].wait()
    for c in last:
        c.wait()

    for b in range(3):
        hi, lo = halves(e_in[:, :, b * 128 : b * 128 + 128].reshape(128, 128).T)
        for ryl in range(4):
            at = (slice(24 * b, 24 * b + 24), slice(128 * ryl, 128 * ryl + 128))
            yh[at] = hi[24 * ryl : 24 * ryl + 24]
            yl[at] = lo[24 * ryl : 24 * ryl + 24]
    y = mm(yh[...], my[0]) + mm(yl[...], my[0]) + mm(yh[...], my[1])
    for b in range(3):
        for a in range(3):
            for k in range(4):
                out[k, 3 * a + b] = y[24 * b + 8 * a : 24 * b + 8 * a + 8, 128 * k : 128 * k + 128]


def body(green, bos_weight, vertex, block_order, window_start):
    mats = [
        first_matrix(-1.0, 1.0),
        second_matrix(-1.0, 1.0, False),
        first_matrix(1.0, 1.0 / L),
        second_matrix(1.0, 1.0 / L, True),
        out_x_matrix(),
        out_y_matrix(),
    ]
    vm = pl.BlockSpec(memory_space=pltpu.VMEM)
    sm = pl.BlockSpec(memory_space=pltpu.SMEM)
    hbm = pl.BlockSpec(memory_space=pl.ANY)
    dma = pltpu.SemaphoreType.DMA
    out = pl.pallas_call(
        whole_kernel,
        out_shape=jax.ShapeDtypeStruct((4, 9, 8, 128), F32),
        in_specs=[sm, sm, vm, vm, vm] + [hbm] * 6,
        out_specs=vm,
        scratch_shapes=[pltpu.VMEM(m.shape, BF16) for m in mats]
        + [
            pltpu.VMEM((2, 9, BOS, 4, 128), BF16),
            pltpu.VMEM((8, 128), F32),
            pltpu.VMEM((BOS, 8, 128), F32),
            pltpu.VMEM((8, 128), F32),
            pltpu.VMEM((L, 2, 5, 128), F32),
            pltpu.VMEM((L, 2, 5, 128), F32),
            pltpu.VMEM((L, 2, 5, 128), F32),
            pltpu.VMEM((128, 5, 128), F32),
            pltpu.VMEM((128, 5, 128), F32),
            pltpu.VMEM((128, 5, 128), F32),
            pltpu.VMEM((9, 128, 128), F32),
            pltpu.VMEM((5, 128, 128), F32),
            pltpu.VMEM((2, 768, 256), BF16),
            pltpu.VMEM((64, 128), F32),
            pltpu.VMEM((2, 768, 768), BF16),
            pltpu.VMEM((2, 768, 768), BF16),
            pltpu.VMEM((2, 8, 48, 128), F32),
            pltpu.VMEM((FER, 2, 3, 8, 128), F32),
            pltpu.VMEM((FER, 2, 3, 8, 128), F32),
            pltpu.VMEM((128, 512), BF16),
            pltpu.VMEM((128, 512), BF16),
            pltpu.VMEM((BOS, 8, 384), F32),
            pltpu.VMEM((BOS, 8, 384), F32),
            pltpu.VMEM((72, 512), BF16),
            pltpu.VMEM((72, 512), BF16),
            dma((6,)), dma((2, BOS)), dma((2, BOS)), dma((BOS,)), dma((BOS,)), dma((3,)), dma((3,)), dma((4,)),
            dma((FER,)), dma((FER,)), dma((BOS,)), dma((BOS,)), pltpu.SemaphoreType.REGULAR,
        ],
        compiler_params=pltpu.CompilerParams(
            has_side_effects=True, collective_id=0, vmem_limit_bytes=VMEM_LIMIT
        ),
        name="dual_self_energy",
    )(
        block_order,
        window_start,
        green.reshape(2, 2, 8, 9, 4, 128),
        bos_weight.reshape(8, 576, 128),
        vertex,
        *[jnp.asarray(m) for m in (mats[0], mats[1], mats[2], mats[3], mats[4], mats[5])],
    )
    return out.transpose(0, 2, 1, 3)


def solution(mesh):
    return jax.shard_map(
        body,
        mesh=mesh,
        in_specs=(
            P(None, "fer", None, "bos", None),
            P("bos", None, None, None),
            P("fer", "bos"),
            P(),
            P(),
        ),
        out_specs=P("bos", "fer", None, None),
        check_vma=False,
    )
```

```python
import functools
import math

import jax
import jax.numpy as jnp
import ml_dtypes
import numpy as np
from jax import lax
from jax.experimental import pallas as pl
from jax.experimental.pallas import tpu as pltpu
from jax.sharding import PartitionSpec as P

MESH = pl.DeviceIdType.MESH
BF16 = jnp.bfloat16
F32 = jnp.float32
L = 64
FER = 8
BOS = 16
VMEM_LIMIT = 56 * 1024 * 1024


def split_np(m):
    hi = m.astype(ml_dtypes.bfloat16)
    lo = (m - hi.astype(np.float64)).astype(ml_dtypes.bfloat16)
    return np.stack([hi, lo])


def trig(a, b):
    t = 2.0 * math.pi * ((np.asarray(a)[:, None] * np.asarray(b)[None, :]) % L) / L
    return np.cos(t), np.sin(t)


def complex_map(c, s, sign):
    m = np.zeros((2, 2) + c.shape)
    m[0, 0], m[1, 1] = c, c
    m[1, 0], m[0, 1] = -sign * s, sign * s
    return m


def first_matrix(sign, scale):
    c, s = trig(np.arange(L), np.arange(L))
    m = complex_map(c, s, sign) * scale
    return split_np(m.transpose(1, 3, 0, 2).reshape(2 * L, 2 * L))


def second_matrix(sign, scale, grouped):
    c, s = trig(np.arange(L), np.arange(L))
    m = complex_map(c, s, sign) * scale
    m = m.reshape(2, 2, L, 2, 2, 16)
    full = np.zeros((2, 2, L, 2, 2, 2, 2, 16))
    for pair in range(2):
        full[:, pair, :, :, :, pair] = m.transpose(0, 2, 3, 4, 1, 5)
    if not grouped:
        full = full.transpose(0, 1, 2, 3, 5, 6, 4, 7)
    return split_np(full.reshape(4 * L, 4 * L))


def out_x_matrix():
    c, s = trig(np.arange(L), np.arange(L))
    m = complex_map(c, s, 1.0) * (-1.0 / L)
    m = m.reshape(2, 2, 2, 2, 16, 16, 4)
    full = np.zeros((3, 16, 2, 4, 2, 2, 4, 2, 16))
    for b in range(3):
        full[b, :, :, :, :, :, b] = m.transpose(5, 1, 6, 2, 3, 0, 4)
    return split_np(full.reshape(3, 128, 512))


def out_y_matrix():
    c, s = trig(np.arange(L), np.arange(L))
    m = complex_map(c, s, 1.0) / L
    m = m.reshape(2, 2, 16, 4, L)
    full = np.zeros((4, 16, 2, 4, 4, 2, L))
    for k in range(4):
        full[:, :, :, k, k] = m.transpose(3, 2, 0, 1, 4)
    return split_np(full.reshape(512, 512))


def mm(a, b):
    return jnp.dot(a, b, preferred_element_type=F32)


def nt(a, b):
    return lax.dot_general(a, b, (((1,), (1,)), ((), ())), preferred_element_type=F32)


def halves(x):
    hi = x.astype(BF16)
    return hi, (x - hi.astype(F32)).astype(BF16)


def hops(offset):
    return sum(min(d, 4 - d) for d in offset[:3]) + 0.5 * offset[3]


FAR_FIRST = sorted(
    [(z, y, x, c) for z in range(4) for y in range(4) for x in range(4) for c in range(2)][1:],
    key=hops,
    reverse=True,
)


def ring(axis, size, start):
    me = lax.axis_index(axis)
    copies = []
    for i in range(1, size):
        to = lax.rem(me + i, size)
        copies.append(
            pltpu.make_async_remote_copy(device_id={axis: to}, device_id_type=MESH, **start(to, i))
        )
    return copies


def transform(x, m1, m2, s_ref, row):
    z = nt(m1[0], x) + nt(m1[1], x)
    hi, lo = halves(jnp.concatenate([z[:L], z[L:]], axis=1))
    y = mm(hi, m2[0]) + mm(hi, m2[1]) + mm(lo, m2[0])
    for half in range(2):
        s_ref[:, half, row, :] = y[:, half * 128 : half * 128 + 128]


def whole_kernel(
    bo, ws, green, weight, vertex, g1h, g2h, w1h, w2h, mxh, myh, out,
    g1, g2, w1, w2, mx, my, planes, vsend, vgot, vsum, sa, sb, sw, ra_in, rb_in, rw_in,
    gt, wk, wb, vert, h0, h1, rows, octets, b_in, lh, ll, quads, e_in, yh, yl,
    csem, green_s, green_r, vert_s, vert_r, pos_s, pos_r, own, oct_s, oct_r, quad_s, quad_r, seen,
):
    f, j = lax.axis_index("fer"), lax.axis_index("bos")
    me = j * FER + f
    place = (j // 8) * 64 + f * 8 + lax.rem(j, 8)
    count = FER * BOS

    barrier = pltpu.get_barrier_semaphore()
    for axis, size, mine in (("bos", BOS, j), ("fer", FER, f)):
        for i in range(1, size):
            pl.semaphore_signal(
                barrier, inc=1, device_id={axis: lax.rem(mine + i, size)}, device_id_type=MESH
            )
    loads = [
        pltpu.make_async_copy(a, b, csem.at[i])
        for i, (a, b) in enumerate(
            ((w1h, w1), (w2h, w2), (g1h, g1), (g2h, g2), (mxh, mx), (myh, my))
        )
    ]
    for c in loads:
        c.start()

    loads[0].wait()
    loads[1].wait()
    for k in range(5):
        if k < 4:
            x = weight[f, 128 * k : 128 * k + 128]
        else:
            x = jnp.concatenate([weight[f, 512:576], jnp.zeros((64, 128), BF16)], axis=0)
        transform(x, w1, w2, sw, k)
    lane8 = lax.broadcasted_iota(jnp.int32, (8, 128), 1)
    spread = jnp.concatenate([vertex[...]] * BOS, axis=1)
    vsend[...] = jnp.where(lane8 // 8 == bo[j], spread, 0.0)

    pl.semaphore_wait(barrier, BOS + FER - 2)
    for i in range(1, FER):
        pl.semaphore_signal(seen, inc=1, device_id={"fer": lax.rem(f + i, FER)}, device_id_type=MESH)

    parts = (pl.ds(0, 3), pl.ds(3, 6))
    near = [
        ring(
            "bos", BOS,
            lambda to, i, h=h: dict(
                src_ref=green.at[:, to // 8, lax.rem(to, 8), parts[h]],
                dst_ref=planes.at[:, parts[h], j],
                send_sem=green_s.at[h, i], recv_sem=green_r.at[h, i],
            ),
        )
        for h in range(2)
    ]
    near[0] += ring(
        "bos", BOS,
        lambda to, i: dict(
            src_ref=vsend, dst_ref=vgot.at[j], send_sem=vert_s.at[i], recv_sem=vert_r.at[i]
        ),
    )
    for c in near[0] + near[1]:
        c.start()
    kept = pltpu.make_async_copy(green.at[:, j // 8, lax.rem(j, 8)], planes.at[:, :, j], own.at[0])
    kept.start()
    vgot[j] = vsend[...]

    pl.semaphore_wait(seen, FER - 1)

    def everywhere(src, dst, which):
        mine = pltpu.make_async_copy(src.at[me // 2, lax.rem(me, 2)], dst.at[place], own.at[1 + which])
        mine.start()

        for dz, dy, dx, dc in FAR_FIRST:
            x = lax.rem(lax.rem(j // 2, 4) + dx, 4)
            y = lax.rem(lax.rem(f, 2) * 2 + j // 8 + dy, 4)
            z = lax.rem(f // 2 + dz, 4)
            fi = z * 2 + y // 2
            ji = lax.rem(y, 2) * 8 + x * 2 + lax.rem(lax.rem(j, 2) + dc, 2)
            pltpu.make_async_remote_copy(
                src_ref=src.at[ji * 4 + fi // 2, lax.rem(fi, 2)],
                dst_ref=dst.at[place],
                send_sem=pos_s.at[which],
                recv_sem=pos_r.at[which],
                device_id={"fer": fi, "bos": ji},
                device_id_type=MESH,
            ).start()
        return mine

    def arrived(dst, which):
        part = dst.at[pl.ds(0, count - 1)]
        pltpu.make_async_remote_copy(
            src_ref=part, dst_ref=part, send_sem=pos_s.at[which], recv_sem=pos_r.at[which],
            device_id={"bos": lax.rem(j + 1, BOS)}, device_id_type=MESH,
        ).wait()

    mine_w = everywhere(sw, rw_in, 0)

    kept.wait()
    loads[2].wait()
    loads[3].wait()

    def planes_of(ac):
        return jnp.concatenate([planes[n2, ac].reshape(L, 128) for n2 in range(2)], axis=0)

    for c in near[0]:
        c.wait()
    total = vgot[0]
    for i in range(1, BOS):
        total = total + vgot[i]
    vsum[...] = total
    sa[:, :, 3, :] = jnp.broadcast_to(
        vsum[pl.ds(lax.rem(j, 8), 1), :].reshape(1, 1, 128), (L, 2, 128)
    )
    for ac in range(3):
        transform(planes_of(ac), g1, g2, sa, ac)
    mine_a = everywhere(sa, ra_in, 1)
    for c in near[1]:
        c.wait()
    for ac in range(3, 9):
        transform(planes_of(ac), g1, g2, sb, ac - 3)
    mine_b = everywhere(sb, rb_in, 2)

    mine_w.wait()
    arrived(rw_in, 0)
    lane = lax.broadcasted_iota(jnp.int32, (128, 128), 1)
    sub = lax.broadcasted_iota(jnp.int32, (128, 128), 0)
    target = jnp.zeros((8, 128), jnp.int32)
    owner = (lane8 // 64) * 8 + lane8 % 8
    for i in range(BOS):
        target = jnp.where(owner == i, bo[i] * 8, target)
    target = target + lane8 // 8 % 8
    target = jnp.concatenate([target] * 16, axis=0)
    for par in range(2):
        order = jnp.where((sub ^ par) == target, 1.0, 0.0).astype(BF16)
        for k in range(5):
            hi, lo = halves(rw_in[:, k, :])
            wk[par, k] = mm(order, hi) + mm(order, lo)
    for par in range(2):
        for rg in range(2):
            for c in range(3):
                t = jnp.zeros((128, 128), F32)
                for b in range(3):
                    k, odd = divmod(3 * c + b, 2)
                    by = (32 * b - 64 * rg - 32 * odd) % 128
                    piece = pltpu.roll(wk[par, k], by, axis=1) if by else wk[par, k]
                    t = jnp.where(lane // 32 == b, piece, t)
                turned = jnp.where(lane % 32 < 16, -pltpu.roll(t, 112, axis=1), pltpu.roll(t, 16, axis=1))
                for ri, part in enumerate((t, turned)):
                    hi, lo = halves(part)
                    at = slice((2 * c + ri) * 128, (2 * c + ri) * 128 + 128)
                    wb[par, rg, at, 0:128] = hi
                    wb[par, rg, at, 128:256] = lo

    s = ws[0]
    lane16 = lax.broadcasted_iota(jnp.int32, (16, 128), 1)
    odd16 = lane16 % 2 == 1

    def octet(t):
        u = lax.rem(t, 4)
        dz = jnp.where(u == 3, 0, jnp.where(u == 2, 3, 2 - u))
        return lax.rem(f // 2 + dz, 4) * 2 + lax.rem(f + 1 + t // 4, 2)

    def build(units, h_ref):
        for n, (t, a) in enumerate(units):
            base = 8 * octet(t)
            shifts = [s + base + 2 * u for u in range(5)]
            upper = [lane16 >= by for by in shifts]
            back = [lax.rem(128 - by, 128) for by in shifts]
            row = [
                jnp.broadcast_to(vert[vi % 2, pl.ds(base + vi, 1), :], (16, 128)) for vi in range(8)
            ]
            for rg in range(2):
                for cr in range(6):
                    ac, at = 3 * a + cr // 2, (cr % 2) * 32 + rg * 16
                    low, high = gt[ac, at : at + 16, :], gt[ac, 64 + at : 80 + at, :]
                    tile = [
                        pltpu.roll(jnp.where(upper[u], low, high), back[u], axis=1) for u in range(5)
                    ]
                    cols = slice(cr * 128, cr * 128 + 128)
                    for u in range(4):
                        for par in range(2):
                            y = jnp.where(odd16, tile[u], tile[u + 1]) if par else tile[u]
                            hi, lo = halves(y * row[2 * u + par])
                            to = (2 * u + n) * 16
                            h_ref[par, rg, to : to + 16, cols] = hi
                            h_ref[par, rg, 128 + to : 144 + to, cols] = lo

    def multiply(units, h_ref):
        for rg in range(2):
            for par in range(2):
                acc = mm(h_ref[par, rg], wb[par, rg])
                acc = acc[:128] + acc[128:]
                acc = (acc[:, :128] + acc[:, 128:]).reshape(4, 32, 128)
                for u in range(4):
                    rows[rg, 2 * u + par] = acc[u]
            for n, (t, a) in enumerate(units):
                o = jnp.zeros((8, 128), F32)
                for r16 in range(16):
                    o = jnp.where(lane8 % 16 == r16, rows[rg, :, n * 16 + r16, :], o)
                octets[t, rg, a] = o

    def pass_on(t):
        return pltpu.make_async_remote_copy(
            src_ref=octets.at[t], dst_ref=b_in.at[f],
            send_sem=oct_s.at[t], recv_sem=oct_r.at[t],
            device_id={"fer": octet(t)}, device_id_type=MESH,
        )

    def first(t):
        return [(2 * t, 0), (2 * t + 1, 0)]

    def others(t):
        return [(t, 1), (t, 2)]

    mine_a.wait()
    arrived(ra_in, 1)
    for ac in range(3):
        gt[ac] = ra_in[:, ac, :].T
    v = ra_in[0:64, 3, :]
    vert[0] = v
    lane64 = lax.broadcasted_iota(jnp.int32, (64, 128), 1)
    vert[1] = jnp.where(lane64 % 2 == 0, pltpu.roll(v, 127, axis=1), pltpu.roll(v, 1, axis=1))

    build(first(0), h0)

    def pair_first(t, carry):
        build(first(2 * t + 1), h1)
        multiply(first(2 * t), h0)
        build(first(jnp.minimum(2 * t + 2, 3)), h0)
        multiply(first(2 * t + 1), h1)
        return carry

    lax.fori_loop(0, 2, pair_first, 0)

    mine_b.wait()
    arrived(rb_in, 2)
    for ac in range(3, 9):
        gt[ac] = rb_in[:, ac - 3, :].T
    build(others(0), h0)

    def pair(t, carry):
        build(others(2 * t + 1), h1)
        multiply(others(2 * t), h0)
        pass_on(2 * t).start()
        build(others(jnp.minimum(2 * t + 2, 7)), h0)
        multiply(others(2 * t + 1), h1)

        @pl.when(t < 3)
        def _():
            pass_on(2 * t + 1).start()

        return carry

    lax.fori_loop(0, 4, pair, 0)
    b_in[f] = octets[7]
    for t in range(7):
        pass_on(t).wait()

    lh[96:, :] = jnp.zeros((32, 512), BF16)
    ll[96:, :] = jnp.zeros((32, 512), BF16)
    for ryl in range(4):
        for half in range(2):
            for rg in range(2):
                hi, lo = halves(b_in[2 * ryl + half, rg].reshape(24, 128))
                at = (
                    slice(24 * ryl, 24 * ryl + 24),
                    slice((2 * half + rg) * 128, (2 * half + rg) * 128 + 128),
                )
                lh[at] = hi
                ll[at] = lo
    loads[4].wait()
    for b in range(3):
        y = nt(mx[0, b], lh[...]) + nt(mx[0, b], ll[...]) + nt(mx[1, b], lh[...])
        quads[:, :, b * 128 : b * 128 + 128] = y.reshape(BOS, 8, 128)
    last = ring(
        "bos", BOS,
        lambda to, i: dict(
            src_ref=quads.at[to], dst_ref=e_in.at[j], send_sem=quad_s.at[i], recv_sem=quad_r.at[i]
        ),
    )
    for c in last:
        c.start()
    e_in[j] = quads[j]
    loads[5].wait()
    for c in last:
        c.wait()

    for b in range(3):
        hi, lo = halves(e_in[:, :, b * 128 : b * 128 + 128].reshape(128, 128).T)
        for ryl in range(4):
            at = (slice(24 * b, 24 * b + 24), slice(128 * ryl, 128 * ryl + 128))
            yh[at] = hi[24 * ryl : 24 * ryl + 24]
            yl[at] = lo[24 * ryl : 24 * ryl + 24]
    y = mm(yh[...], my[0]) + mm(yl[...], my[0]) + mm(yh[...], my[1])
    for b in range(3):
        for a in range(3):
            for k in range(4):
                out[k, 3 * a + b] = y[24 * b + 8 * a : 24 * b + 8 * a + 8, 128 * k : 128 * k + 128]


def body(green, bos_weight, vertex, block_order, window_start):
    mats = [
        first_matrix(-1.0, 1.0),
        second_matrix(-1.0, 1.0, False),
        first_matrix(1.0, 1.0 / L),
        second_matrix(1.0, 1.0 / L, True),
        out_x_matrix(),
        out_y_matrix(),
    ]
    vm = pl.BlockSpec(memory_space=pltpu.VMEM)
    sm = pl.BlockSpec(memory_space=pltpu.SMEM)
    hbm = pl.BlockSpec(memory_space=pl.ANY)
    dma = pltpu.SemaphoreType.DMA
    out = pl.pallas_call(
        whole_kernel,
        out_shape=jax.ShapeDtypeStruct((4, 9, 8, 128), F32),
        in_specs=[sm, sm, vm, vm, vm] + [hbm] * 6,
        out_specs=vm,
        scratch_shapes=[pltpu.VMEM(m.shape, BF16) for m in mats]
        + [
            pltpu.VMEM((2, 9, BOS, 4, 128), BF16),
            pltpu.VMEM((8, 128), F32),
            pltpu.VMEM((BOS, 8, 128), F32),
            pltpu.VMEM((8, 128), F32),
            pltpu.VMEM((L, 2, 4, 128), F32),
            pltpu.VMEM((L, 2, 6, 128), F32),
            pltpu.VMEM((L, 2, 5, 128), F32),
            pltpu.VMEM((128, 4, 128), F32),
            pltpu.VMEM((128, 6, 128), F32),
            pltpu.VMEM((128, 5, 128), F32),
            pltpu.VMEM((9, 128, 128), F32),
            pltpu.VMEM((2, 5, 128, 128), F32),
            pltpu.VMEM((2, 2, 768, 256), BF16),
            pltpu.VMEM((2, 64, 128), F32),
            pltpu.VMEM((2, 2, 256, 768), BF16),
            pltpu.VMEM((2, 2, 256, 768), BF16),
            pltpu.VMEM((2, 8, 32, 128), F32),
            pltpu.VMEM((FER, 2, 3, 8, 128), F32),
            pltpu.VMEM((FER, 2, 3, 8, 128), F32),
            pltpu.VMEM((128, 512), BF16),
            pltpu.VMEM((128, 512), BF16),
            pltpu.VMEM((BOS, 8, 384), F32),
            pltpu.VMEM((BOS, 8, 384), F32),
            pltpu.VMEM((72, 512), BF16),
            pltpu.VMEM((72, 512), BF16),
            dma((6,)), dma((2, BOS)), dma((2, BOS)), dma((BOS,)), dma((BOS,)), dma((3,)), dma((3,)), dma((4,)),
            dma((FER,)), dma((FER,)), dma((BOS,)), dma((BOS,)), pltpu.SemaphoreType.REGULAR,
        ],
        compiler_params=pltpu.CompilerParams(
            has_side_effects=True, collective_id=0, vmem_limit_bytes=VMEM_LIMIT
        ),
        name="dual_self_energy",
    )(
        block_order,
        window_start,
        green.reshape(2, 2, 8, 9, 4, 128),
        bos_weight.reshape(8, 576, 128),
        vertex,
        *[jnp.asarray(m) for m in (mats[0], mats[1], mats[2], mats[3], mats[4], mats[5])],
    )
    return out.transpose(0, 2, 1, 3)


def solution(mesh):
    return jax.shard_map(
        body,
        mesh=mesh,
        in_specs=(
            P(None, "fer", None, "bos", None),
            P("bos", None, None, None),
            P("fer", "bos"),
            P(),
            P(),
        ),
        out_specs=P("bos", "fer", None, None),
        check_vma=False,
    )
```

```python
import functools
import math

import jax
import jax.numpy as jnp
import ml_dtypes
import numpy as np
from jax import lax
from jax.experimental import pallas as pl
from jax.experimental.pallas import tpu as pltpu
from jax.sharding import PartitionSpec as P

MESH = pl.DeviceIdType.MESH
BF16 = jnp.bfloat16
F32 = jnp.float32
L = 64
FER = 8
BOS = 16
VMEM_LIMIT = 56 * 1024 * 1024


def split_np(m):
    hi = m.astype(ml_dtypes.bfloat16)
    lo = (m - hi.astype(np.float64)).astype(ml_dtypes.bfloat16)
    return np.stack([hi, lo])


def trig(a, b):
    t = 2.0 * math.pi * ((np.asarray(a)[:, None] * np.asarray(b)[None, :]) % L) / L
    return np.cos(t), np.sin(t)


def complex_map(c, s, sign):
    m = np.zeros((2, 2) + c.shape)
    m[0, 0], m[1, 1] = c, c
    m[1, 0], m[0, 1] = -sign * s, sign * s
    return m


def first_matrix(sign, scale):
    c, s = trig(np.arange(L), np.arange(L))
    m = complex_map(c, s, sign) * scale
    return split_np(m.transpose(1, 3, 0, 2).reshape(2 * L, 2 * L))


def second_matrix(sign, scale, grouped):
    c, s = trig(np.arange(L), np.arange(L))
    m = complex_map(c, s, sign) * scale
    m = m.reshape(2, 2, L, 2, 2, 16)
    full = np.zeros((2, 2, L, 2, 2, 2, 2, 16))
    for pair in range(2):
        full[:, pair, :, :, :, pair] = m.transpose(0, 2, 3, 4, 1, 5)
    if not grouped:
        full = full.transpose(0, 1, 2, 3, 5, 6, 4, 7)
    return split_np(full.reshape(4 * L, 4 * L))


def out_x_matrix():
    c, s = trig(np.arange(L), np.arange(L))
    m = complex_map(c, s, 1.0) * (-1.0 / L)
    m = m.reshape(2, 2, 2, 2, 16, 16, 4)
    full = np.zeros((3, 16, 2, 4, 2, 2, 4, 2, 16))
    for b in range(3):
        full[b, :, :, :, :, :, b] = m.transpose(5, 1, 6, 2, 3, 0, 4)
    return split_np(full.reshape(3, 128, 512))


def out_y_matrix():
    c, s = trig(np.arange(L), np.arange(L))
    m = complex_map(c, s, 1.0) / L
    m = m.reshape(2, 2, 16, 4, L)
    full = np.zeros((4, 16, 2, 4, 4, 2, L))
    for k in range(4):
        full[:, :, :, k, k] = m.transpose(3, 2, 0, 1, 4)
    return split_np(full.reshape(512, 512))


def mm(a, b):
    return jnp.dot(a, b, preferred_element_type=F32)


def nt(a, b):
    return lax.dot_general(a, b, (((1,), (1,)), ((), ())), preferred_element_type=F32)


def halves(x):
    hi = x.astype(BF16)
    return hi, (x - hi.astype(F32)).astype(BF16)


def hops(offset):
    return sum(min(d, 4 - d) for d in offset[:3]) + 0.5 * offset[3]


FAR_FIRST = sorted(
    [(z, y, x, c) for z in range(4) for y in range(4) for x in range(4) for c in range(2)][1:],
    key=hops,
    reverse=True,
)


def rows_ring(j, start):
    copies = []
    for i, (_, y, x, c) in enumerate(o for o in FAR_FIRST if o[0] == 0 and o[1] < 2):
        to = (
            lax.rem(j // 8 + y, 2) * 8
            + lax.rem(lax.rem(j // 2, 4) + x, 4) * 2
            + lax.rem(lax.rem(j, 2) + c, 2)
        )
        copies.append(
            pltpu.make_async_remote_copy(device_id={"bos": to}, device_id_type=MESH, **start(to, i))
        )
    return copies


def transform(x, m1, m2, s_ref, row, more=None):
    z = nt(m1[0], x) + nt(m1[1], x)
    hi, lo = halves(jnp.concatenate([z[:L], z[L:]], axis=1))
    y = mm(hi, m2[0]) + mm(hi, m2[1]) + mm(lo, m2[0])
    for half in range(2):
        part = y[:, half * 128 : half * 128 + 128]
        s_ref[:, half, row, :] = part if more is None else part + more


def vertex_lane(vi):
    return 32 + 8 * vi if vi < 4 else 64 + 8 * vi


def whole_kernel(
    bo, ws, green, weight, vertex, g1h, g2h, w1h, w2h, mxh, myh, out,
    g1, g2, w1, w2, mx, my, planes, wx, sa, sb, sw, ra_in, rb_in, rw_in,
    gt, wk, wb, vert, h0, h1, rows, octets, b_in, lh, ll, quads, e_in, yh, yl,
    csem, green_s, green_r, pos_s, pos_r, own, oct_s, oct_r, quad_s, quad_r, seen,
):
    f, j = lax.axis_index("fer"), lax.axis_index("bos")
    me = j * FER + f
    place = (j // 8) * 64 + f * 8 + lax.rem(j, 8)
    count = FER * BOS

    barrier = pltpu.get_barrier_semaphore()
    for axis, size, mine in (("bos", BOS, j), ("fer", FER, f)):
        for i in range(1, size):
            pl.semaphore_signal(
                barrier, inc=1, device_id={axis: lax.rem(mine + i, size)}, device_id_type=MESH
            )
    loads = [
        pltpu.make_async_copy(a, b, csem.at[i])
        for i, (a, b) in enumerate(
            (
                (w1h, w1), (w2h, w2), (g1h, g1), (g2h, g2), (mxh, mx), (myh, my), (weight.at[f], wx),
            )
        )
    ]
    for i in (6, 0, 1, 2, 3, 4, 5):
        loads[i].start()

    lane8 = lax.broadcasted_iota(jnp.int32, (8, 128), 1)
    wide = jnp.concatenate([vertex[...], jnp.zeros((8, 120), F32)], axis=1)
    values = jnp.zeros((1, 128), F32)
    for vi in range(8):
        at = vertex_lane(vi)
        moved = pltpu.roll(jnp.broadcast_to(wide[vi : vi + 1], (8, 128)), at, axis=1)
        values = jnp.where(lane8[:1] // 8 == at // 8, moved[:1], values)
    loads[6].wait()
    loads[0].wait()
    loads[1].wait()
    for k in range(4):
        transform(wx[128 * k : 128 * k + 128], w1, w2, sw, k)
    x = jnp.concatenate([wx[512:576], jnp.zeros((64, 128), BF16)], axis=0)
    transform(x, w1, w2, sw, 4, values)

    pl.semaphore_wait(barrier, BOS + FER - 2)
    for i in range(1, FER):
        pl.semaphore_signal(seen, inc=1, device_id={"fer": lax.rem(f + i, FER)}, device_id_type=MESH)

    parts = (pl.ds(0, 3), pl.ds(3, 6))
    near = [
        rows_ring(
            j,
            lambda to, i, h=h: dict(
                src_ref=green.at[:, to // 8, lax.rem(to, 8), parts[h]],
                dst_ref=planes.at[:, parts[h], j],
                send_sem=green_s.at[h, i], recv_sem=green_r.at[h, i],
            ),
        )
        for h in range(2)
    ]
    for c in near[0] + near[1]:
        c.start()
    kept = pltpu.make_async_copy(green.at[:, j // 8, lax.rem(j, 8)], planes.at[:, :, j], own.at[0])
    kept.start()

    pl.semaphore_wait(seen, FER - 1)

    def everywhere(src, dst, which):
        mine = pltpu.make_async_copy(src.at[me // 2, lax.rem(me, 2)], dst.at[place], own.at[1 + which])
        mine.start()

        for dz, dy, dx, dc in FAR_FIRST:
            x = lax.rem(lax.rem(j // 2, 4) + dx, 4)
            y = lax.rem(lax.rem(f, 2) * 2 + j // 8 + dy, 4)
            z = lax.rem(f // 2 + dz, 4)
            fi = z * 2 + y // 2
            ji = lax.rem(y, 2) * 8 + x * 2 + lax.rem(lax.rem(j, 2) + dc, 2)
            pltpu.make_async_remote_copy(
                src_ref=src.at[ji * 4 + fi // 2, lax.rem(fi, 2)],
                dst_ref=dst.at[place],
                send_sem=pos_s.at[which],
                recv_sem=pos_r.at[which],
                device_id={"fer": fi, "bos": ji},
                device_id_type=MESH,
            ).start()
        return mine

    def arrived(dst, which):
        part = dst.at[pl.ds(0, count - 1)]
        pltpu.make_async_remote_copy(
            src_ref=part, dst_ref=part, send_sem=pos_s.at[which], recv_sem=pos_r.at[which],
            device_id={"bos": lax.rem(j + 1, BOS)}, device_id_type=MESH,
        ).wait()

    mine_w = everywhere(sw, rw_in, 0)

    kept.wait()
    loads[2].wait()
    loads[3].wait()

    def planes_of(ac):
        return jnp.concatenate([planes[n2, ac].reshape(L, 128) for n2 in range(2)], axis=0)

    for c in near[0]:
        c.wait()
    for ac in range(3):
        transform(planes_of(ac), g1, g2, sa, ac)
    mine_a = everywhere(sa, ra_in, 1)
    for c in near[1]:
        c.wait()
    for ac in range(3, 9):
        transform(planes_of(ac), g1, g2, sb, ac - 3)
    mine_b = everywhere(sb, rb_in, 2)

    mine_w.wait()
    arrived(rw_in, 0)
    lane = lax.broadcasted_iota(jnp.int32, (128, 128), 1)
    sub = lax.broadcasted_iota(jnp.int32, (128, 128), 0)
    target = jnp.zeros((8, 128), jnp.int32)
    owner = (lane8 // 64) * 8 + lane8 % 8
    for i in range(BOS):
        target = jnp.where(owner == i, bo[i] * 8, target)
    target = target + lane8 // 8 % 8
    target = jnp.concatenate([target] * 16, axis=0)
    for par in range(2):
        order = jnp.where((sub ^ par) == target, 1.0, 0.0).astype(BF16)
        for k in range(5):
            hi, lo = halves(rw_in[:, k, :])
            wk[par, k] = mm(order, hi) + mm(order, lo)
    for par in range(2):
        for rg in range(2):
            for c in range(3):
                t = jnp.zeros((128, 128), F32)
                for b in range(3):
                    k, odd = divmod(3 * c + b, 2)
                    by = (32 * b - 64 * rg - 32 * odd) % 128
                    piece = pltpu.roll(wk[par, k], by, axis=1) if by else wk[par, k]
                    t = jnp.where(lane // 32 == b, piece, t)
                turned = jnp.where(lane % 32 < 16, -pltpu.roll(t, 112, axis=1), pltpu.roll(t, 16, axis=1))
                for ri, part in enumerate((t, turned)):
                    hi, lo = halves(part)
                    at = slice((2 * c + ri) * 128, (2 * c + ri) * 128 + 128)
                    wb[par, rg, at, 0:128] = hi
                    wb[par, rg, at, 128:256] = lo

    table = [jnp.zeros((8, 128), F32) for _ in range(8)]
    for i in range(BOS):
        x = rw_in[pl.ds((i // 8) * 64 + i % 8, 8, stride=8), 4, :]
        for vi in range(8):
            moved = pltpu.roll(x, lax.rem(8 * bo[i] - vertex_lane(vi) + 128, 128), axis=1)
            table[vi] = jnp.where(lane8 // 8 == bo[i], moved, table[vi])
    for vi in range(8):
        vert[0, pl.ds(vi, 8, stride=8), :] = table[vi]
    v = vert[0]
    lane64 = lax.broadcasted_iota(jnp.int32, (64, 128), 1)
    vert[1] = jnp.where(lane64 % 2 == 0, pltpu.roll(v, 127, axis=1), pltpu.roll(v, 1, axis=1))

    s = ws[0]
    lane16 = lax.broadcasted_iota(jnp.int32, (16, 128), 1)
    odd16 = lane16 % 2 == 1

    def octet(t):
        u = lax.rem(t, 4)
        dz = jnp.where(u == 3, 0, jnp.where(u == 2, 3, 2 - u))
        return lax.rem(f // 2 + dz, 4) * 2 + lax.rem(f + 1 + t // 4, 2)

    def build(units, h_ref):
        for n, (t, a) in enumerate(units):
            base = 8 * octet(t)
            shifts = [s + base + 2 * u for u in range(5)]
            upper = [lane16 >= by for by in shifts]
            back = [lax.rem(128 - by, 128) for by in shifts]
            row = [
                jnp.broadcast_to(vert[vi % 2, pl.ds(base + vi, 1), :], (16, 128)) for vi in range(8)
            ]
            for rg in range(2):
                for cr in range(6):
                    ac, at = 3 * a + cr // 2, (cr % 2) * 32 + rg * 16
                    low, high = gt[ac, at : at + 16, :], gt[ac, 64 + at : 80 + at, :]
                    tile = [
                        pltpu.roll(jnp.where(upper[u], low, high), back[u], axis=1) for u in range(5)
                    ]
                    cols = slice(cr * 128, cr * 128 + 128)
                    for u in range(4):
                        for par in range(2):
                            y = jnp.where(odd16, tile[u], tile[u + 1]) if par else tile[u]
                            hi, lo = halves(y * row[2 * u + par])
                            to = (2 * u + n) * 16
                            h_ref[par, rg, to : to + 16, cols] = hi
                            h_ref[par, rg, 128 + to : 144 + to, cols] = lo

    def multiply(units, h_ref):
        for rg in range(2):
            for par in range(2):
                acc = mm(h_ref[par, rg], wb[par, rg])
                acc = acc[:128] + acc[128:]
                acc = (acc[:, :128] + acc[:, 128:]).reshape(4, 32, 128)
                for u in range(4):
                    rows[rg, 2 * u + par] = acc[u]
            for n, (t, a) in enumerate(units):
                o = jnp.zeros((8, 128), F32)
                for r16 in range(16):
                    o = jnp.where(lane8 % 16 == r16, rows[rg, :, n * 16 + r16, :], o)
                octets[t, rg, a] = o

    def pass_on(t):
        return pltpu.make_async_remote_copy(
            src_ref=octets.at[t], dst_ref=b_in.at[f],
            send_sem=oct_s.at[t], recv_sem=oct_r.at[t],
            device_id={"fer": octet(t)}, device_id_type=MESH,
        )

    def first(t):
        return [(2 * t, 0), (2 * t + 1, 0)]

    def others(t):
        return [(t, 1), (t, 2)]

    mine_a.wait()
    arrived(ra_in, 1)
    for ac in range(3):
        gt[ac] = ra_in[:, ac, :].T

    build(first(0), h0)

    def pair_first(t, carry):
        build(first(2 * t + 1), h1)
        multiply(first(2 * t), h0)
        build(first(jnp.minimum(2 * t + 2, 3)), h0)
        multiply(first(2 * t + 1), h1)
        return carry

    lax.fori_loop(0, 2, pair_first, 0)

    mine_b.wait()
    arrived(rb_in, 2)
    for ac in range(3, 9):
        gt[ac] = rb_in[:, ac - 3, :].T
    build(others(0), h0)

    def pair(t, carry):
        build(others(2 * t + 1), h1)
        multiply(others(2 * t), h0)
        pass_on(2 * t).start()
        build(others(jnp.minimum(2 * t + 2, 7)), h0)
        multiply(others(2 * t + 1), h1)

        @pl.when(t < 3)
        def _():
            pass_on(2 * t + 1).start()

        return carry

    lax.fori_loop(0, 4, pair, 0)
    b_in[f] = octets[7]
    for t in range(7):
        pass_on(t).wait()

    lh[96:, :] = jnp.zeros((32, 512), BF16)
    ll[96:, :] = jnp.zeros((32, 512), BF16)
    for ryl in range(4):
        for half in range(2):
            for rg in range(2):
                hi, lo = halves(b_in[2 * ryl + half, rg].reshape(24, 128))
                at = (
                    slice(24 * ryl, 24 * ryl + 24),
                    slice((2 * half + rg) * 128, (2 * half + rg) * 128 + 128),
                )
                lh[at] = hi
                ll[at] = lo
    loads[4].wait()
    for b in range(3):
        y = nt(mx[0, b], lh[...]) + nt(mx[0, b], ll[...]) + nt(mx[1, b], lh[...])
        quads[:, :, b * 128 : b * 128 + 128] = y.reshape(BOS, 8, 128)
    last = rows_ring(
        j,
        lambda to, i: dict(
            src_ref=quads.at[to], dst_ref=e_in.at[j], send_sem=quad_s.at[i], recv_sem=quad_r.at[i]
        ),
    )
    for c in last:
        c.start()
    e_in[j] = quads[j]
    loads[5].wait()
    for c in last:
        c.wait()

    for b in range(3):
        hi, lo = halves(e_in[:, :, b * 128 : b * 128 + 128].reshape(128, 128).T)
        for ryl in range(4):
            at = (slice(24 * b, 24 * b + 24), slice(128 * ryl, 128 * ryl + 128))
            yh[at] = hi[24 * ryl : 24 * ryl + 24]
            yl[at] = lo[24 * ryl : 24 * ryl + 24]
    y = mm(yh[...], my[0]) + mm(yl[...], my[0]) + mm(yh[...], my[1])
    for b in range(3):
        for a in range(3):
            for k in range(4):
                out[k, 3 * a + b] = y[24 * b + 8 * a : 24 * b + 8 * a + 8, 128 * k : 128 * k + 128]


def body(green, bos_weight, vertex, block_order, window_start):
    mats = [
        first_matrix(-1.0, 1.0),
        second_matrix(-1.0, 1.0, False),
        first_matrix(1.0, 1.0 / L),
        second_matrix(1.0, 1.0 / L, True),
        out_x_matrix(),
        out_y_matrix(),
    ]
    vm = pl.BlockSpec(memory_space=pltpu.VMEM)
    sm = pl.BlockSpec(memory_space=pltpu.SMEM)
    hbm = pl.BlockSpec(memory_space=pl.ANY)
    dma = pltpu.SemaphoreType.DMA
    out = pl.pallas_call(
        whole_kernel,
        out_shape=jax.ShapeDtypeStruct((4, 9, 8, 128), F32),
        in_specs=[sm, sm, hbm, hbm, vm] + [hbm] * 6,
        out_specs=vm,
        scratch_shapes=[pltpu.VMEM(m.shape, BF16) for m in mats]
        + [
            pltpu.VMEM((2, 9, BOS, 4, 128), BF16),
            pltpu.VMEM((576, 128), BF16),
            pltpu.VMEM((L, 2, 3, 128), F32),
            pltpu.VMEM((L, 2, 6, 128), F32),
            pltpu.VMEM((L, 2, 5, 128), F32),
            pltpu.VMEM((128, 3, 128), F32),
            pltpu.VMEM((128, 6, 128), F32),
            pltpu.VMEM((128, 5, 128), F32),
            pltpu.VMEM((9, 128, 128), F32),
            pltpu.VMEM((2, 5, 128, 128), F32),
            pltpu.VMEM((2, 2, 768, 256), BF16),
            pltpu.VMEM((2, 64, 128), F32),
            pltpu.VMEM((2, 2, 256, 768), BF16),
            pltpu.VMEM((2, 2, 256, 768), BF16),
            pltpu.VMEM((2, 8, 32, 128), F32),
            pltpu.VMEM((FER, 2, 3, 8, 128), F32),
            pltpu.VMEM((FER, 2, 3, 8, 128), F32),
            pltpu.VMEM((128, 512), BF16),
            pltpu.VMEM((128, 512), BF16),
            pltpu.VMEM((BOS, 8, 384), F32),
            pltpu.VMEM((BOS, 8, 384), F32),
            pltpu.VMEM((72, 512), BF16),
            pltpu.VMEM((72, 512), BF16),
            dma((7,)), dma((2, BOS)), dma((2, BOS)), dma((3,)), dma((3,)), dma((4,)),
            dma((FER,)), dma((FER,)), dma((BOS,)), dma((BOS,)), pltpu.SemaphoreType.REGULAR,
        ],
        compiler_params=pltpu.CompilerParams(
            has_side_effects=True, collective_id=0, vmem_limit_bytes=VMEM_LIMIT
        ),
        name="dual_self_energy",
    )(
        block_order,
        window_start,
        green.reshape(2, 2, 8, 9, 4, 128),
        bos_weight.reshape(8, 576, 128),
        vertex,
        *[jnp.asarray(m) for m in (mats[0], mats[1], mats[2], mats[3], mats[4], mats[5])],
    )
    return out.transpose(0, 2, 1, 3)


def solution(mesh):
    return jax.shard_map(
        body,
        mesh=mesh,
        in_specs=(
            P(None, "fer", None, "bos", None),
            P("bos", None, None, None),
            P("fer", "bos"),
            P(),
            P(),
        ),
        out_specs=P("bos", "fer", None, None),
        check_vma=False,
    )
```

```python
import functools
import math

import jax
import jax.numpy as jnp
import ml_dtypes
import numpy as np
from jax import lax
from jax.experimental import pallas as pl
from jax.experimental.pallas import tpu as pltpu
from jax.sharding import PartitionSpec as P

MESH = pl.DeviceIdType.MESH
BF16 = jnp.bfloat16
F32 = jnp.float32
L = 64
FER = 8
BOS = 16
VMEM_LIMIT = 56 * 1024 * 1024


def split_np(m):
    hi = m.astype(ml_dtypes.bfloat16)
    lo = (m - hi.astype(np.float64)).astype(ml_dtypes.bfloat16)
    return np.stack([hi, lo])


def trig(a, b):
    t = 2.0 * math.pi * ((np.asarray(a)[:, None] * np.asarray(b)[None, :]) % L) / L
    return np.cos(t), np.sin(t)


def complex_map(c, s, sign):
    m = np.zeros((2, 2) + c.shape)
    m[0, 0], m[1, 1] = c, c
    m[1, 0], m[0, 1] = -sign * s, sign * s
    return m


def first_matrix(sign, scale):
    c, s = trig(np.arange(L), np.arange(L))
    m = complex_map(c, s, sign) * scale
    return split_np(m.transpose(1, 3, 0, 2).reshape(2 * L, 2 * L))


def second_matrix(sign, scale, grouped):
    c, s = trig(np.arange(L), np.arange(L))
    m = complex_map(c, s, sign) * scale
    m = m.reshape(2, 2, L, 2, 2, 16)
    full = np.zeros((2, 2, L, 2, 2, 2, 2, 16))
    for pair in range(2):
        full[:, pair, :, :, :, pair] = m.transpose(0, 2, 3, 4, 1, 5)
    if not grouped:
        full = full.transpose(0, 1, 2, 3, 5, 6, 4, 7)
    return split_np(full.reshape(4 * L, 4 * L))


def out_x_matrix():
    c, s = trig(np.arange(L), np.arange(L))
    m = complex_map(c, s, 1.0) * (-1.0 / L)
    m = m.reshape(2, 2, 2, 2, 16, 16, 4)
    full = np.zeros((3, 16, 2, 4, 2, 2, 4, 2, 16))
    for b in range(3):
        full[b, :, :, :, :, :, b] = m.transpose(5, 1, 6, 2, 3, 0, 4)
    return split_np(full.reshape(3, 128, 512))


def out_y_matrix():
    c, s = trig(np.arange(L), np.arange(L))
    m = complex_map(c, s, 1.0) / L
    m = m.reshape(2, 2, 16, 4, L)
    full = np.zeros((4, 16, 2, 4, 4, 2, L))
    for k in range(4):
        full[:, :, :, k, k] = m.transpose(3, 2, 0, 1, 4)
    return split_np(full.reshape(512, 512))


def mm(a, b):
    return jnp.dot(a, b, preferred_element_type=F32)


def nt(a, b):
    return lax.dot_general(a, b, (((1,), (1,)), ((), ())), preferred_element_type=F32)


def halves(x):
    hi = x.astype(BF16)
    return hi, (x - hi.astype(F32)).astype(BF16)


def hops(offset):
    return sum(min(d, 4 - d) for d in offset[:3]) + 0.5 * offset[3]


FAR_FIRST = sorted(
    [(z, y, x, c) for z in range(4) for y in range(4) for x in range(4) for c in range(2)][1:],
    key=hops,
    reverse=True,
)


def octet_of(f, t):
    u = lax.rem(t, 4)
    dz = jnp.where(u == 3, 0, jnp.where(u == 2, 3, 2 - u))
    return lax.rem(f // 2 + dz, 4) * 2 + lax.rem(f + 1 + t // 4, 2)


def rows_order(j):
    return [
        lax.rem(j // 8 + y, 2) * 8
        + lax.rem(lax.rem(j // 2, 4) + x, 4) * 2
        + lax.rem(lax.rem(j, 2) + c, 2)
        for _, y, x, c in FAR_FIRST
        if _ == 0 and y < 2
    ]


def rows_ring(j, start):
    return [
        pltpu.make_async_remote_copy(device_id={"bos": to}, device_id_type=MESH, **start(to, i))
        for i, to in enumerate(rows_order(j))
    ]


def transform(x, m1, m2, s_ref, row, more=None):
    z = nt(m1[0], x) + nt(m1[1], x)
    hi, lo = halves(jnp.concatenate([z[:L], z[L:]], axis=1))
    y = mm(hi, m2[0]) + mm(hi, m2[1]) + mm(lo, m2[0])
    for half in range(2):
        part = y[:, half * 128 : half * 128 + 128]
        s_ref[:, half, row, :] = part if more is None else part + more


def vertex_lane(vi):
    return 32 + 8 * vi if vi < 4 else 64 + 8 * vi


def whole_kernel(
    bo, ws, green, weight, vertex, g1h, g2h, w1h, w2h, mxh, myh, out,
    g1, g2, w1, w2, mx, my, planes, wx, sa, sb, sw, ra_in, rb_in, rw_in,
    gt, wk, wb, vert, h0, h1, rows, octets, b_in, lh, ll, quads, e_in, yh, yl,
    csem, green_s, green_r, pos_s, pos_r, own, oct_s, oct_r, quad_s, quad_r, seen,
):
    f, j = lax.axis_index("fer"), lax.axis_index("bos")
    me = j * FER + f
    place = (j // 8) * 64 + f * 8 + lax.rem(j, 8)
    count = FER * BOS

    barrier = pltpu.get_barrier_semaphore()
    for to in [octet_of(f, t) for t in range(FER - 1)]:
        pl.semaphore_signal(barrier, inc=1, device_id={"fer": to}, device_id_type=MESH)
    for to in rows_order(j):
        pl.semaphore_signal(barrier, inc=1, device_id={"bos": to}, device_id_type=MESH)
    loads = [
        pltpu.make_async_copy(a, b, csem.at[i])
        for i, (a, b) in enumerate(
            (
                (w1h, w1), (w2h, w2), (g1h, g1), (g2h, g2), (mxh, mx), (myh, my), (weight.at[f], wx),
            )
        )
    ]
    for i in (6, 0, 1, 2, 3, 4, 5):
        loads[i].start()

    lane8 = lax.broadcasted_iota(jnp.int32, (8, 128), 1)
    wide = jnp.concatenate([vertex[...], jnp.zeros((8, 120), F32)], axis=1)
    values = jnp.zeros((1, 128), F32)
    for vi in range(8):
        at = vertex_lane(vi)
        moved = pltpu.roll(jnp.broadcast_to(wide[vi : vi + 1], (8, 128)), at, axis=1)
        values = jnp.where(lane8[:1] // 8 == at // 8, moved[:1], values)
    loads[6].wait()
    loads[0].wait()
    loads[1].wait()
    for k in range(4):
        transform(wx[128 * k : 128 * k + 128], w1, w2, sw, k)
    x = jnp.concatenate([wx[512:576], jnp.zeros((64, 128), BF16)], axis=0)
    transform(x, w1, w2, sw, 4, values)

    pl.semaphore_wait(barrier, BOS + FER - 2)
    for i in range(1, FER):
        pl.semaphore_signal(seen, inc=1, device_id={"fer": lax.rem(f + i, FER)}, device_id_type=MESH)

    parts = (pl.ds(0, 3), pl.ds(3, 6))
    near = [
        rows_ring(
            j,
            lambda to, i, h=h: dict(
                src_ref=green.at[:, to // 8, lax.rem(to, 8), parts[h]],
                dst_ref=planes.at[:, parts[h], j],
                send_sem=green_s.at[h, i], recv_sem=green_r.at[h, i],
            ),
        )
        for h in range(2)
    ]
    for c in near[0] + near[1]:
        c.start()
    kept = pltpu.make_async_copy(green.at[:, j // 8, lax.rem(j, 8)], planes.at[:, :, j], own.at[0])
    kept.start()

    pl.semaphore_wait(seen, FER - 1)

    def everywhere(src, dst, which):
        mine = pltpu.make_async_copy(src.at[me // 2, lax.rem(me, 2)], dst.at[place], own.at[1 + which])
        mine.start()

        for dz, dy, dx, dc in FAR_FIRST:
            x = lax.rem(lax.rem(j // 2, 4) + dx, 4)
            y = lax.rem(lax.rem(f, 2) * 2 + j // 8 + dy, 4)
            z = lax.rem(f // 2 + dz, 4)
            fi = z * 2 + y // 2
            ji = lax.rem(y, 2) * 8 + x * 2 + lax.rem(lax.rem(j, 2) + dc, 2)
            pltpu.make_async_remote_copy(
                src_ref=src.at[ji * 4 + fi // 2, lax.rem(fi, 2)],
                dst_ref=dst.at[place],
                send_sem=pos_s.at[which],
                recv_sem=pos_r.at[which],
                device_id={"fer": fi, "bos": ji},
                device_id_type=MESH,
            ).start()
        return mine

    def arrived(dst, which):
        part = dst.at[pl.ds(0, count - 1)]
        pltpu.make_async_remote_copy(
            src_ref=part, dst_ref=part, send_sem=pos_s.at[which], recv_sem=pos_r.at[which],
            device_id={"bos": lax.rem(j + 1, BOS)}, device_id_type=MESH,
        ).wait()

    mine_w = everywhere(sw, rw_in, 0)

    kept.wait()
    loads[2].wait()
    loads[3].wait()

    def planes_of(ac):
        return jnp.concatenate([planes[n2, ac].reshape(L, 128) for n2 in range(2)], axis=0)

    for c in near[0]:
        c.wait()
    for ac in range(3):
        transform(planes_of(ac), g1, g2, sa, ac)
    mine_a = everywhere(sa, ra_in, 1)
    for c in near[1]:
        c.wait()
    for ac in range(3, 9):
        transform(planes_of(ac), g1, g2, sb, ac - 3)
    mine_b = everywhere(sb, rb_in, 2)

    mine_w.wait()
    arrived(rw_in, 0)
    lane = lax.broadcasted_iota(jnp.int32, (128, 128), 1)
    sub = lax.broadcasted_iota(jnp.int32, (128, 128), 0)
    target = jnp.zeros((8, 128), jnp.int32)
    owner = (lane8 // 64) * 8 + lane8 % 8
    for i in range(BOS):
        target = jnp.where(owner == i, bo[i] * 8, target)
    target = target + lane8 // 8 % 8
    target = jnp.concatenate([target] * 16, axis=0)
    for par in range(2):
        order = jnp.where((sub ^ par) == target, 1.0, 0.0).astype(BF16)
        for k in range(5):
            hi, lo = halves(rw_in[:, k, :])
            wk[par, k] = mm(order, hi) + mm(order, lo)
    for par in range(2):
        for rg in range(2):
            for c in range(3):
                t = jnp.zeros((128, 128), F32)
                for b in range(3):
                    k, odd = divmod(3 * c + b, 2)
                    by = (32 * b - 64 * rg - 32 * odd) % 128
                    piece = pltpu.roll(wk[par, k], by, axis=1) if by else wk[par, k]
                    t = jnp.where(lane // 32 == b, piece, t)
                turned = jnp.where(lane % 32 < 16, -pltpu.roll(t, 112, axis=1), pltpu.roll(t, 16, axis=1))
                for ri, part in enumerate((t, turned)):
                    hi, lo = halves(part)
                    at = slice((2 * c + ri) * 128, (2 * c + ri) * 128 + 128)
                    wb[par, rg, at, 0:128] = hi
                    wb[par, rg, at, 128:256] = lo

    table = [jnp.zeros((8, 128), F32) for _ in range(8)]
    for i in range(BOS):
        x = rw_in[pl.ds((i // 8) * 64 + i % 8, 8, stride=8), 4, :]
        for vi in range(8):
            moved = pltpu.roll(x, lax.rem(8 * bo[i] - vertex_lane(vi) + 128, 128), axis=1)
            table[vi] = jnp.where(lane8 // 8 == bo[i], moved, table[vi])
    for vi in range(8):
        vert[0, pl.ds(vi, 8, stride=8), :] = table[vi]
    v = vert[0]
    lane64 = lax.broadcasted_iota(jnp.int32, (64, 128), 1)
    vert[1] = jnp.where(lane64 % 2 == 0, pltpu.roll(v, 127, axis=1), pltpu.roll(v, 1, axis=1))

    s = ws[0]
    lane16 = lax.broadcasted_iota(jnp.int32, (16, 128), 1)
    odd16 = lane16 % 2 == 1

    def octet(t):
        return octet_of(f, t)

    def build(units, h_ref):
        for n, (t, a) in enumerate(units):
            base = 8 * octet(t)
            shifts = [s + base + 2 * u for u in range(5)]
            upper = [lane16 >= by for by in shifts]
            back = [lax.rem(128 - by, 128) for by in shifts]
            row = [
                jnp.broadcast_to(vert[vi % 2, pl.ds(base + vi, 1), :], (16, 128)) for vi in range(8)
            ]
            for rg in range(2):
                for cr in range(6):
                    ac, at = 3 * a + cr // 2, (cr % 2) * 32 + rg * 16
                    low, high = gt[ac, at : at + 16, :], gt[ac, 64 + at : 80 + at, :]
                    tile = [
                        pltpu.roll(jnp.where(upper[u], low, high), back[u], axis=1) for u in range(5)
                    ]
                    cols = slice(cr * 128, cr * 128 + 128)
                    for u in range(4):
                        for par in range(2):
                            y = jnp.where(odd16, tile[u], tile[u + 1]) if par else tile[u]
                            hi, lo = halves(y * row[2 * u + par])
                            to = (2 * u + n) * 16
                            h_ref[par, rg, to : to + 16, cols] = hi
                            h_ref[par, rg, 128 + to : 144 + to, cols] = lo

    def multiply(units, h_ref):
        for rg in range(2):
            for par in range(2):
                acc = mm(h_ref[par, rg], wb[par, rg])
                acc = acc[:128] + acc[128:]
                acc = (acc[:, :128] + acc[:, 128:]).reshape(4, 32, 128)
                for u in range(4):
                    rows[rg, 2 * u + par] = acc[u]
            for n, (t, a) in enumerate(units):
                o = jnp.zeros((8, 128), F32)
                for r16 in range(16):
                    o = jnp.where(lane8 % 16 == r16, rows[rg, :, n * 16 + r16, :], o)
                octets[t, rg, a] = o

    def pass_on(t):
        return pltpu.make_async_remote_copy(
            src_ref=octets.at[t], dst_ref=b_in.at[f],
            send_sem=oct_s.at[t], recv_sem=oct_r.at[t],
            device_id={"fer": octet(t)}, device_id_type=MESH,
        )

    def first(t):
        return [(2 * t, 0), (2 * t + 1, 0)]

    def others(t):
        return [(t, 1), (t, 2)]

    mine_a.wait()
    arrived(ra_in, 1)
    for ac in range(3):
        gt[ac] = ra_in[:, ac, :].T

    build(first(0), h0)

    def pair_first(t, carry):
        build(first(2 * t + 1), h1)
        multiply(first(2 * t), h0)
        build(first(jnp.minimum(2 * t + 2, 3)), h0)
        multiply(first(2 * t + 1), h1)
        return carry

    lax.fori_loop(0, 2, pair_first, 0)

    mine_b.wait()
    arrived(rb_in, 2)
    for ac in range(3, 9):
        gt[ac] = rb_in[:, ac - 3, :].T
    build(others(0), h0)

    def pair(t, carry):
        build(others(2 * t + 1), h1)
        multiply(others(2 * t), h0)
        build(others(2 * t + 2), h0)
        multiply(others(2 * t + 1), h1)
        pass_on(2 * t).start()
        pass_on(2 * t + 1).start()
        return carry

    lax.fori_loop(0, 3, pair, 0)
    build(others(7), h1)
    multiply(others(6), h0)
    pass_on(6).start()
    multiply(others(7), h1)
    b_in[f] = octets[7]
    for t in range(7):
        pass_on(t).wait()

    lh[96:, :] = jnp.zeros((32, 512), BF16)
    ll[96:, :] = jnp.zeros((32, 512), BF16)
    for ryl in range(4):
        for half in range(2):
            for rg in range(2):
                hi, lo = halves(b_in[2 * ryl + half, rg].reshape(24, 128))
                at = (
                    slice(24 * ryl, 24 * ryl + 24),
                    slice((2 * half + rg) * 128, (2 * half + rg) * 128 + 128),
                )
                lh[at] = hi
                ll[at] = lo
    loads[4].wait()
    for b in range(3):
        y = nt(mx[0, b], lh[...]) + nt(mx[0, b], ll[...]) + nt(mx[1, b], lh[...])
        quads[:, :, b * 128 : b * 128 + 128] = y.reshape(BOS, 8, 128)
    last = rows_ring(
        j,
        lambda to, i: dict(
            src_ref=quads.at[to], dst_ref=e_in.at[j], send_sem=quad_s.at[i], recv_sem=quad_r.at[i]
        ),
    )
    for c in last:
        c.start()
    e_in[j] = quads[j]
    loads[5].wait()
    for c in last:
        c.wait()

    for b in range(3):
        hi, lo = halves(e_in[:, :, b * 128 : b * 128 + 128].reshape(128, 128).T)
        for ryl in range(4):
            at = (slice(24 * b, 24 * b + 24), slice(128 * ryl, 128 * ryl + 128))
            yh[at] = hi[24 * ryl : 24 * ryl + 24]
            yl[at] = lo[24 * ryl : 24 * ryl + 24]
    y = mm(yh[...], my[0]) + mm(yl[...], my[0]) + mm(yh[...], my[1])
    for b in range(3):
        for a in range(3):
            for k in range(4):
                out[k, 3 * a + b] = y[24 * b + 8 * a : 24 * b + 8 * a + 8, 128 * k : 128 * k + 128]


def body(green, bos_weight, vertex, block_order, window_start):
    mats = [
        first_matrix(-1.0, 1.0),
        second_matrix(-1.0, 1.0, False),
        first_matrix(1.0, 1.0 / L),
        second_matrix(1.0, 1.0 / L, True),
        out_x_matrix(),
        out_y_matrix(),
    ]
    vm = pl.BlockSpec(memory_space=pltpu.VMEM)
    sm = pl.BlockSpec(memory_space=pltpu.SMEM)
    hbm = pl.BlockSpec(memory_space=pl.ANY)
    dma = pltpu.SemaphoreType.DMA
    out = pl.pallas_call(
        whole_kernel,
        out_shape=jax.ShapeDtypeStruct((4, 9, 8, 128), F32),
        in_specs=[sm, sm, hbm, hbm, vm] + [hbm] * 6,
        out_specs=vm,
        scratch_shapes=[pltpu.VMEM(m.shape, BF16) for m in mats]
        + [
            pltpu.VMEM((2, 9, BOS, 4, 128), BF16),
            pltpu.VMEM((576, 128), BF16),
            pltpu.VMEM((L, 2, 3, 128), F32),
            pltpu.VMEM((L, 2, 6, 128), F32),
            pltpu.VMEM((L, 2, 5, 128), F32),
            pltpu.VMEM((128, 3, 128), F32),
            pltpu.VMEM((128, 6, 128), F32),
            pltpu.VMEM((128, 5, 128), F32),
            pltpu.VMEM((9, 128, 128), F32),
            pltpu.VMEM((2, 5, 128, 128), F32),
            pltpu.VMEM((2, 2, 768, 256), BF16),
            pltpu.VMEM((2, 64, 128), F32),
            pltpu.VMEM((2, 2, 256, 768), BF16),
            pltpu.VMEM((2, 2, 256, 768), BF16),
            pltpu.VMEM((2, 8, 32, 128), F32),
            pltpu.VMEM((FER, 2, 3, 8, 128), F32),
            pltpu.VMEM((FER, 2, 3, 8, 128), F32),
            pltpu.VMEM((128, 512), BF16),
            pltpu.VMEM((128, 512), BF16),
            pltpu.VMEM((BOS, 8, 384), F32),
            pltpu.VMEM((BOS, 8, 384), F32),
            pltpu.VMEM((72, 512), BF16),
            pltpu.VMEM((72, 512), BF16),
            dma((7,)), dma((2, BOS)), dma((2, BOS)), dma((3,)), dma((3,)), dma((4,)),
            dma((FER,)), dma((FER,)), dma((BOS,)), dma((BOS,)), pltpu.SemaphoreType.REGULAR,
        ],
        compiler_params=pltpu.CompilerParams(
            has_side_effects=True, collective_id=0, vmem_limit_bytes=VMEM_LIMIT
        ),
        name="dual_self_energy",
    )(
        block_order,
        window_start,
        green.reshape(2, 2, 8, 9, 4, 128),
        bos_weight.reshape(8, 576, 128),
        vertex,
        *[jnp.asarray(m) for m in (mats[0], mats[1], mats[2], mats[3], mats[4], mats[5])],
    )
    return out.transpose(0, 2, 1, 3)


def solution(mesh):
    return jax.shard_map(
        body,
        mesh=mesh,
        in_specs=(
            P(None, "fer", None, "bos", None),
            P("bos", None, None, None),
            P("fer", "bos"),
            P(),
            P(),
        ),
        out_specs=P("bos", "fer", None, None),
        check_vma=False,
    )
```

```python
import functools
import math

import jax
import jax.numpy as jnp
import ml_dtypes
import numpy as np
from jax import lax
from jax.experimental import pallas as pl
from jax.experimental.pallas import tpu as pltpu
from jax.sharding import PartitionSpec as P

MESH = pl.DeviceIdType.MESH
BF16 = jnp.bfloat16
F32 = jnp.float32
L = 64
FER = 8
BOS = 16
VMEM_LIMIT = 56 * 1024 * 1024


def split_np(m):
    hi = m.astype(ml_dtypes.bfloat16)
    lo = (m - hi.astype(np.float64)).astype(ml_dtypes.bfloat16)
    return np.stack([hi, lo])


def trig(a, b):
    t = 2.0 * math.pi * ((np.asarray(a)[:, None] * np.asarray(b)[None, :]) % L) / L
    return np.cos(t), np.sin(t)


def complex_map(c, s, sign):
    m = np.zeros((2, 2) + c.shape)
    m[0, 0], m[1, 1] = c, c
    m[1, 0], m[0, 1] = -sign * s, sign * s
    return m


def first_matrix(sign, scale):
    c, s = trig(np.arange(L), np.arange(L))
    m = complex_map(c, s, sign) * scale
    return split_np(m.transpose(1, 3, 0, 2).reshape(2 * L, 2 * L))


def second_matrix(sign, scale, grouped):
    c, s = trig(np.arange(L), np.arange(L))
    m = complex_map(c, s, sign) * scale
    m = m.reshape(2, 2, L, 2, 2, 16)
    full = np.zeros((2, 2, L, 2, 2, 2, 2, 16))
    for pair in range(2):
        full[:, pair, :, :, :, pair] = m.transpose(0, 2, 3, 4, 1, 5)
    if not grouped:
        full = full.transpose(0, 1, 2, 3, 5, 6, 4, 7)
    return split_np(full.reshape(4 * L, 4 * L))


def out_x_matrix():
    c, s = trig(np.arange(L), np.arange(L))
    m = complex_map(c, s, 1.0) * (-1.0 / L)
    m = m.reshape(2, 2, 2, 2, 16, 16, 4)
    full = np.zeros((3, 16, 2, 4, 2, 2, 4, 2, 16))
    for b in range(3):
        full[b, :, :, :, :, :, b] = m.transpose(5, 1, 6, 2, 3, 0, 4)
    return split_np(full.reshape(3, 128, 512))


def out_y_matrix():
    c, s = trig(np.arange(L), np.arange(L))
    m = complex_map(c, s, 1.0) / L
    m = m.reshape(2, 2, 16, 4, L)
    full = np.zeros((4, 16, 2, 4, 4, 2, L))
    for k in range(4):
        full[:, :, :, k, k] = m.transpose(3, 2, 0, 1, 4)
    return split_np(full.reshape(512, 512))


def mm(a, b):
    return jnp.dot(a, b, preferred_element_type=F32)


def nt(a, b):
    return lax.dot_general(a, b, (((1,), (1,)), ((), ())), preferred_element_type=F32)


def halves(x):
    hi = x.astype(BF16)
    return hi, (x - hi.astype(F32)).astype(BF16)


def hops(offset):
    return sum(min(d, 4 - d) for d in offset[:3]) + 0.5 * offset[3]


FAR_FIRST = sorted(
    [(z, y, x, c) for z in range(4) for y in range(4) for x in range(4) for c in range(2)][1:],
    key=hops,
    reverse=True,
)


def octet_of(f, t):
    u = lax.rem(t, 4)
    dz = jnp.where(u == 3, 0, jnp.where(u == 2, 3, 2 - u))
    return lax.rem(f // 2 + dz, 4) * 2 + lax.rem(f + 1 + t // 4, 2)


def rows_order(j):
    return [
        lax.rem(j // 8 + y, 2) * 8
        + lax.rem(lax.rem(j // 2, 4) + x, 4) * 2
        + lax.rem(lax.rem(j, 2) + c, 2)
        for _, y, x, c in FAR_FIRST
        if _ == 0 and y < 2
    ]


def rows_ring(j, start):
    return [
        pltpu.make_async_remote_copy(device_id={"bos": to}, device_id_type=MESH, **start(to, i))
        for i, to in enumerate(rows_order(j))
    ]


def transform(x, m1, m2, s_ref, row, more=None):
    z = nt(m1[0], x) + nt(m1[1], x)
    hi, lo = halves(jnp.concatenate([z[:L], z[L:]], axis=1))
    y = mm(hi, m2[0]) + mm(hi, m2[1]) + mm(lo, m2[0])
    for half in range(2):
        part = y[:, half * 128 : half * 128 + 128]
        s_ref[:, half, row, :] = part if more is None else part + more


def vertex_lane(vi):
    return 32 + 8 * vi if vi < 4 else 64 + 8 * vi


def whole_kernel(
    boh, wsh, green, weight, vertex, g1h, g2h, w1h, w2h, mxh, myh, out,
    g1, g2, w1, w2, mx, my, planes, wx, sa, sb, sw, ra_in, rb_in, rw_in,
    gt, wk, wb, vert, h0, h1, rows, octets, b_in, lh, ll, quads, e_in, yh, yl,
    csem, green_s, green_r, pos_s, pos_r, own, oct_s, oct_r, quad_s, quad_r, seen, bo, ws,
):
    f, j = lax.axis_index("fer"), lax.axis_index("bos")
    me = j * FER + f
    place = (j // 8) * 64 + f * 8 + lax.rem(j, 8)
    count = FER * BOS

    barrier = pltpu.get_barrier_semaphore()
    for to in [octet_of(f, t) for t in range(FER - 1)]:
        pl.semaphore_signal(barrier, inc=1, device_id={"fer": to}, device_id_type=MESH)
    for to in rows_order(j):
        pl.semaphore_signal(barrier, inc=1, device_id={"bos": to}, device_id_type=MESH)
    loads = [
        pltpu.make_async_copy(a, b, csem.at[i])
        for i, (a, b) in enumerate(
            (
                (w1h, w1), (w2h, w2), (g1h, g1), (g2h, g2), (mxh, mx), (myh, my), (weight.at[f], wx), (boh, bo), (wsh, ws),
            )
        )
    ]
    for i in (6, 0, 1, 2, 3, 4, 5, 7, 8):
        loads[i].start()

    lane8 = lax.broadcasted_iota(jnp.int32, (8, 128), 1)
    wide = jnp.concatenate([vertex[...], jnp.zeros((8, 120), F32)], axis=1)
    values = jnp.zeros((1, 128), F32)
    for vi in range(8):
        at = vertex_lane(vi)
        moved = pltpu.roll(jnp.broadcast_to(wide[vi : vi + 1], (8, 128)), at, axis=1)
        values = jnp.where(lane8[:1] // 8 == at // 8, moved[:1], values)
    loads[6].wait()
    loads[0].wait()
    loads[1].wait()
    for k in range(4):
        transform(wx[128 * k : 128 * k + 128], w1, w2, sw, k)
    x = jnp.concatenate([wx[512:576], jnp.zeros((64, 128), BF16)], axis=0)
    transform(x, w1, w2, sw, 4, values)

    pl.semaphore_wait(barrier, BOS + FER - 2)
    parts = (pl.ds(0, 3), pl.ds(3, 6))
    near = [
        rows_ring(
            j,
            lambda to, i, h=h: dict(
                src_ref=green.at[:, to // 8, lax.rem(to, 8), parts[h]],
                dst_ref=planes.at[:, parts[h], j],
                send_sem=green_s.at[h, i], recv_sem=green_r.at[h, i],
            ),
        )
        for h in range(2)
    ]
    for c in near[0]:
        c.start()
    for i in range(1, FER):
        pl.semaphore_signal(seen, inc=1, device_id={"fer": lax.rem(f + i, FER)}, device_id_type=MESH)
    for c in near[1]:
        c.start()
    kept = pltpu.make_async_copy(green.at[:, j // 8, lax.rem(j, 8)], planes.at[:, :, j], own.at[0])
    kept.start()

    pl.semaphore_wait(seen, FER - 1)

    def everywhere(src, dst, which):
        mine = pltpu.make_async_copy(src.at[me // 2, lax.rem(me, 2)], dst.at[place], own.at[1 + which])
        mine.start()

        for dz, dy, dx, dc in FAR_FIRST:
            x = lax.rem(lax.rem(j // 2, 4) + dx, 4)
            y = lax.rem(lax.rem(f, 2) * 2 + j // 8 + dy, 4)
            z = lax.rem(f // 2 + dz, 4)
            fi = z * 2 + y // 2
            ji = lax.rem(y, 2) * 8 + x * 2 + lax.rem(lax.rem(j, 2) + dc, 2)
            pltpu.make_async_remote_copy(
                src_ref=src.at[ji * 4 + fi // 2, lax.rem(fi, 2)],
                dst_ref=dst.at[place],
                send_sem=pos_s.at[which],
                recv_sem=pos_r.at[which],
                device_id={"fer": fi, "bos": ji},
                device_id_type=MESH,
            ).start()
        return mine

    def arrived(dst, which):
        part = dst.at[pl.ds(0, count - 1)]
        pltpu.make_async_remote_copy(
            src_ref=part, dst_ref=part, send_sem=pos_s.at[which], recv_sem=pos_r.at[which],
            device_id={"bos": lax.rem(j + 1, BOS)}, device_id_type=MESH,
        ).wait()

    mine_w = everywhere(sw, rw_in, 0)

    kept.wait()
    loads[2].wait()
    loads[3].wait()

    def planes_of(ac):
        return jnp.concatenate([planes[n2, ac].reshape(L, 128) for n2 in range(2)], axis=0)

    for c in near[0]:
        c.wait()
    for ac in range(3):
        transform(planes_of(ac), g1, g2, sa, ac)
    mine_a = everywhere(sa, ra_in, 1)
    for c in near[1]:
        c.wait()
    for ac in range(3, 9):
        transform(planes_of(ac), g1, g2, sb, ac - 3)
    mine_b = everywhere(sb, rb_in, 2)

    loads[7].wait()
    loads[8].wait()
    mine_w.wait()
    arrived(rw_in, 0)
    lane = lax.broadcasted_iota(jnp.int32, (128, 128), 1)
    sub = lax.broadcasted_iota(jnp.int32, (128, 128), 0)
    target = jnp.zeros((8, 128), jnp.int32)
    owner = (lane8 // 64) * 8 + lane8 % 8
    for i in range(BOS):
        target = jnp.where(owner == i, bo[i] * 8, target)
    target = target + lane8 // 8 % 8
    target = jnp.concatenate([target] * 16, axis=0)
    for par in range(2):
        order = jnp.where((sub ^ par) == target, 1.0, 0.0).astype(BF16)
        for k in range(5):
            hi, lo = halves(rw_in[:, k, :])
            wk[par, k] = mm(order, hi) + mm(order, lo)
    for par in range(2):
        for rg in range(2):
            for c in range(3):
                t = jnp.zeros((128, 128), F32)
                for b in range(3):
                    k, odd = divmod(3 * c + b, 2)
                    by = (32 * b - 64 * rg - 32 * odd) % 128
                    piece = pltpu.roll(wk[par, k], by, axis=1) if by else wk[par, k]
                    t = jnp.where(lane // 32 == b, piece, t)
                turned = jnp.where(lane % 32 < 16, -pltpu.roll(t, 112, axis=1), pltpu.roll(t, 16, axis=1))
                for ri, part in enumerate((t, turned)):
                    hi, lo = halves(part)
                    at = slice((2 * c + ri) * 128, (2 * c + ri) * 128 + 128)
                    wb[par, rg, at, 0:128] = hi
                    wb[par, rg, at, 128:256] = lo

    table = [jnp.zeros((8, 128), F32) for _ in range(8)]
    for i in range(BOS):
        x = rw_in[pl.ds((i // 8) * 64 + i % 8, 8, stride=8), 4, :]
        for vi in range(8):
            moved = pltpu.roll(x, lax.rem(8 * bo[i] - vertex_lane(vi) + 128, 128), axis=1)
            table[vi] = jnp.where(lane8 // 8 == bo[i], moved, table[vi])
    for vi in range(8):
        vert[0, pl.ds(vi, 8, stride=8), :] = table[vi]
    v = vert[0]
    lane64 = lax.broadcasted_iota(jnp.int32, (64, 128), 1)
    vert[1] = jnp.where(lane64 % 2 == 0, pltpu.roll(v, 127, axis=1), pltpu.roll(v, 1, axis=1))

    s = ws[0]
    lane16 = lax.broadcasted_iota(jnp.int32, (16, 128), 1)
    odd16 = lane16 % 2 == 1

    def octet(t):
        return octet_of(f, t)

    def build(units, h_ref):
        for n, (t, a) in enumerate(units):
            base = 8 * octet(t)
            shifts = [s + base + 2 * u for u in range(5)]
            upper = [lane16 >= by for by in shifts]
            back = [lax.rem(128 - by, 128) for by in shifts]
            row = [
                jnp.broadcast_to(vert[vi % 2, pl.ds(base + vi, 1), :], (16, 128)) for vi in range(8)
            ]
            for rg in range(2):
                for cr in range(6):
                    ac, at = 3 * a + cr // 2, (cr % 2) * 32 + rg * 16
                    low, high = gt[ac, at : at + 16, :], gt[ac, 64 + at : 80 + at, :]
                    tile = [
                        pltpu.roll(jnp.where(upper[u], low, high), back[u], axis=1) for u in range(5)
                    ]
                    cols = slice(cr * 128, cr * 128 + 128)
                    for u in range(4):
                        for par in range(2):
                            y = jnp.where(odd16, tile[u], tile[u + 1]) if par else tile[u]
                            hi, lo = halves(y * row[2 * u + par])
                            to = (2 * u + n) * 16
                            h_ref[par, rg, to : to + 16, cols] = hi
                            h_ref[par, rg, 128 + to : 144 + to, cols] = lo

    def multiply(units, h_ref):
        for rg in range(2):
            for par in range(2):
                acc = mm(h_ref[par, rg], wb[par, rg])
                acc = acc[:128] + acc[128:]
                acc = (acc[:, :128] + acc[:, 128:]).reshape(4, 32, 128)
                for u in range(4):
                    rows[rg, 2 * u + par] = acc[u]
            for n, (t, a) in enumerate(units):
                o = jnp.zeros((8, 128), F32)
                for r16 in range(16):
                    o = jnp.where(lane8 % 16 == r16, rows[rg, :, n * 16 + r16, :], o)
                octets[t, rg, a] = o

    def pass_on(t):
        return pltpu.make_async_remote_copy(
            src_ref=octets.at[t], dst_ref=b_in.at[f],
            send_sem=oct_s.at[t], recv_sem=oct_r.at[t],
            device_id={"fer": octet(t)}, device_id_type=MESH,
        )

    def first(t):
        return [(2 * t, 0), (2 * t + 1, 0)]

    def others(t):
        return [(t, 1), (t, 2)]

    mine_a.wait()
    arrived(ra_in, 1)
    for ac in range(3):
        gt[ac] = ra_in[:, ac, :].T

    build(first(0), h0)

    def pair_first(t, carry):
        build(first(2 * t + 1), h1)
        multiply(first(2 * t), h0)
        build(first(jnp.minimum(2 * t + 2, 3)), h0)
        multiply(first(2 * t + 1), h1)
        return carry

    lax.fori_loop(0, 2, pair_first, 0)

    mine_b.wait()
    arrived(rb_in, 2)
    for ac in range(3, 9):
        gt[ac] = rb_in[:, ac - 3, :].T
    build(others(0), h0)

    def pair(t, carry):
        build(others(2 * t + 1), h1)
        multiply(others(2 * t), h0)
        build(others(2 * t + 2), h0)
        multiply(others(2 * t + 1), h1)
        pass_on(2 * t).start()
        pass_on(2 * t + 1).start()
        return carry

    lax.fori_loop(0, 3, pair, 0)
    build(others(7), h1)
    multiply(others(6), h0)
    pass_on(6).start()
    multiply(others(7), h1)
    b_in[f] = octets[7]
    for t in range(7):
        pass_on(t).wait()

    lh[96:, :] = jnp.zeros((32, 512), BF16)
    ll[96:, :] = jnp.zeros((32, 512), BF16)
    for ryl in range(4):
        for half in range(2):
            for rg in range(2):
                hi, lo = halves(b_in[2 * ryl + half, rg].reshape(24, 128))
                at = (
                    slice(24 * ryl, 24 * ryl + 24),
                    slice((2 * half + rg) * 128, (2 * half + rg) * 128 + 128),
                )
                lh[at] = hi
                ll[at] = lo
    loads[4].wait()
    for b in range(3):
        y = nt(mx[0, b], lh[...]) + nt(mx[0, b], ll[...]) + nt(mx[1, b], lh[...])
        quads[:, :, b * 128 : b * 128 + 128] = y.reshape(BOS, 8, 128)
    last = rows_ring(
        j,
        lambda to, i: dict(
            src_ref=quads.at[to], dst_ref=e_in.at[j], send_sem=quad_s.at[i], recv_sem=quad_r.at[i]
        ),
    )
    for c in last:
        c.start()
    e_in[j] = quads[j]
    loads[5].wait()
    for c in last:
        c.wait()

    for b in range(3):
        hi, lo = halves(e_in[:, :, b * 128 : b * 128 + 128].reshape(128, 128).T)
        for ryl in range(4):
            at = (slice(24 * b, 24 * b + 24), slice(128 * ryl, 128 * ryl + 128))
            yh[at] = hi[24 * ryl : 24 * ryl + 24]
            yl[at] = lo[24 * ryl : 24 * ryl + 24]
    y = mm(yh[...], my[0]) + mm(yl[...], my[0]) + mm(yh[...], my[1])
    for b in range(3):
        for a in range(3):
            for k in range(4):
                out[k, 3 * a + b] = y[24 * b + 8 * a : 24 * b + 8 * a + 8, 128 * k : 128 * k + 128]


def body(green, bos_weight, vertex, block_order, window_start):
    mats = [
        first_matrix(-1.0, 1.0),
        second_matrix(-1.0, 1.0, False),
        first_matrix(1.0, 1.0 / L),
        second_matrix(1.0, 1.0 / L, True),
        out_x_matrix(),
        out_y_matrix(),
    ]
    vm = pl.BlockSpec(memory_space=pltpu.VMEM)
    hbm = pl.BlockSpec(memory_space=pl.ANY)
    dma = pltpu.SemaphoreType.DMA
    out = pl.pallas_call(
        whole_kernel,
        out_shape=jax.ShapeDtypeStruct((4, 9, 8, 128), F32),
        in_specs=[hbm, hbm, hbm, hbm, vm] + [hbm] * 6,
        out_specs=vm,
        scratch_shapes=[pltpu.VMEM(m.shape, BF16) for m in mats]
        + [
            pltpu.VMEM((2, 9, BOS, 4, 128), BF16),
            pltpu.VMEM((576, 128), BF16),
            pltpu.VMEM((L, 2, 3, 128), F32),
            pltpu.VMEM((L, 2, 6, 128), F32),
            pltpu.VMEM((L, 2, 5, 128), F32),
            pltpu.VMEM((128, 3, 128), F32),
            pltpu.VMEM((128, 6, 128), F32),
            pltpu.VMEM((128, 5, 128), F32),
            pltpu.VMEM((9, 128, 128), F32),
            pltpu.VMEM((2, 5, 128, 128), F32),
            pltpu.VMEM((2, 2, 768, 256), BF16),
            pltpu.VMEM((2, 64, 128), F32),
            pltpu.VMEM((2, 2, 256, 768), BF16),
            pltpu.VMEM((2, 2, 256, 768), BF16),
            pltpu.VMEM((2, 8, 32, 128), F32),
            pltpu.VMEM((FER, 2, 3, 8, 128), F32),
            pltpu.VMEM((FER, 2, 3, 8, 128), F32),
            pltpu.VMEM((128, 512), BF16),
            pltpu.VMEM((128, 512), BF16),
            pltpu.VMEM((BOS, 8, 384), F32),
            pltpu.VMEM((BOS, 8, 384), F32),
            pltpu.VMEM((72, 512), BF16),
            pltpu.VMEM((72, 512), BF16),
            dma((9,)), dma((2, BOS)), dma((2, BOS)), dma((3,)), dma((3,)), dma((4,)),
            dma((FER,)), dma((FER,)), dma((BOS,)), dma((BOS,)), pltpu.SemaphoreType.REGULAR,
            pltpu.SMEM((16,), jnp.int32), pltpu.SMEM((1,), jnp.int32),
        ],
        compiler_params=pltpu.CompilerParams(
            has_side_effects=True, collective_id=0, vmem_limit_bytes=VMEM_LIMIT
        ),
        name="dual_self_energy",
    )(
        block_order,
        window_start,
        green.reshape(2, 2, 8, 9, 4, 128),
        bos_weight.reshape(8, 576, 128),
        vertex,
        *[jnp.asarray(m) for m in (mats[0], mats[1], mats[2], mats[3], mats[4], mats[5])],
    )
    return out.transpose(0, 2, 1, 3)


def solution(mesh):
    return jax.shard_map(
        body,
        mesh=mesh,
        in_specs=(
            P(None, "fer", None, "bos", None),
            P("bos", None, None, None),
            P("fer", "bos"),
            P(),
            P(),
        ),
        out_specs=P("bos", "fer", None, None),
        check_vma=False,
    )
```
